32 devices in a mesh: seqa: 4 (over x, core), seqb: 8 (over z, y).
Axes of the slice: x: 2, y: 2, z: 4, core: 2. Of those that a mesh axis runs over, the one named last changes fastest.
Arguments:
- sequence_input: bfloat16 [16384, 640], P(('seqa', 'seqb')), may hold values from -6 to 6
- w_prev: bfloat16 [3, 640, 1280], P(None, 'seqa'), may hold values from -0.15625 to 0.15625
- w_now: bfloat16 [3, 640, 1280], P(None, 'seqa'), may hold values from -0.15625 to 0.15625
- conv_bias: float32 [3, 1280], replicated, may hold values from -4 to 4
- w_mix: bfloat16 [3, 640, 640], P(None, None, 'seqa'), may hold values from -0.25 to 0.25
Outputs:
- seq_out: bfloat16 [16384, 640], P(('seqa', 'seqb'))
The draws below stay inside these ranges and needn't reach their ends.
All inputs are finite; a program needn't handle non-finite values.
Results may differ from the reference program's by a relative error of at most 0.0052.
Values may be sent and summed in bfloat16 or wider, within the bound.
A program may use at most 64 MiB of HBM per device.

```python
import jax
import jax.numpy as jnp
from jax import lax

D = 640
LAYERS = 3
DILATION_FIRST1 = 128
DILATION_SECOND2 = 512
DILATION_THIRD3 = 2048
TOTAL = 16384


def shard_levels(key, extent, shards, low, largest):
    level, own = 1.0, jax.random.fold_in(key, 6)
    for axis_at, blocks in shards:
        draws = jnp.exp(jax.random.uniform(jax.random.fold_in(own, axis_at), (blocks,), jnp.float32, low / len(shards), largest / len(shards)))
        level = level * jnp.repeat(draws, extent[axis_at] // blocks).reshape([-1 if axis == axis_at else 1 for axis in range(len(extent))])
    return level


def gaussian(rng, shape, width, most, cuts=(), held_as=jnp.bfloat16):
    factor_of = shard_levels(rng, shape, cuts, -0.22, 0.18) if cuts else 1.0
    array = jax.random.normal(rng, shape, jnp.float32) * width * factor_of
    return jnp.minimum(jnp.maximum(array, -most), most).astype(held_as)


def setup_inputs(seed: int = 0) -> dict:
    arg_keys = jax.random.split(jax.random.key(seed), 6)
    sequence_input = gaussian(arg_keys[0], (TOTAL, D), 1.0, 6.0, ((0, 32),))
    w_prev = gaussian(arg_keys[1], (LAYERS, D, 2 * D), (2 * D) ** -0.5, 0.15625, ((1, 4),))
    w_now = gaussian(arg_keys[2], (LAYERS, D, 2 * D), (2 * D) ** -0.5, 0.15625, ((1, 4),))
    conv_bias = gaussian(arg_keys[3], (LAYERS, 2 * D), 1.0, 4.0, (), jnp.float32)
    w_mix = gaussian(arg_keys[4], (LAYERS, D, D), D ** -0.5, 0.25, ((2, 4),))
    return dict(sequence_input=sequence_input, w_prev=w_prev, w_now=w_now, conv_bias=conv_bias, w_mix=w_mix)


def norm_rows(values):
    scale = lax.rsqrt(lax.optimization_barrier(jnp.mean(values * values, axis=1, keepdims=True)) + 1e-06)
    return (values * scale).astype(jnp.bfloat16)

def reference(sequence_input, w_prev, w_now, conv_bias, w_mix):
    hidden_state = sequence_input.astype(jnp.float32)
    for layer_index, dilation_step in enumerate((DILATION_FIRST1, DILATION_SECOND2, DILATION_THIRD3)):
        normed = norm_rows(hidden_state)
        earlier = jnp.pad(normed, ((dilation_step, 0), (0, 0)))[:normed.shape[0]]
        pre = jnp.dot(earlier, w_prev[layer_index], preferred_element_type=jnp.float32)
        pre = pre + jnp.dot(normed, w_now[layer_index], preferred_element_type=jnp.float32)
        pre = pre + conv_bias[layer_index]
        hidden = (pre[:, :D] * jax.nn.sigmoid(pre[:, D:])).astype(jnp.bfloat16)
        hidden_state = hidden_state + jnp.dot(hidden, w_mix[layer_index], preferred_element_type=jnp.float32)
    return hidden_state.astype(jnp.bfloat16)
```

```python
import functools

import jax
import jax.numpy as jnp
from jax import lax
from jax.experimental import pallas as pl
from jax.experimental.pallas import tpu as pltpu
from jax.sharding import PartitionSpec as P

DILATIONS = (128, 512, 2048)
EPS = 1e-06
TILE = 16
GROUP = 4
MESH_ID = pl.DeviceIdType.MESH


def from_behind(value, axis, by):
    peers = lax.axis_size(axis)
    pairs = [(i, i + by) for i in range(peers) if 0 <= i + by < peers]
    return lax.ppermute(value, axis, pairs)


def norm_rows(values):
    scale = lax.rsqrt(jnp.mean(values * values, axis=1, keepdims=True) + EPS)
    return (values * scale).astype(jnp.bfloat16)


def block_prior(normed, dilation_step):
    rows = normed.shape[0]
    whole = dilation_step // rows
    part = dilation_step % rows
    pieces = []
    if part > 0:
        pieces.append(from_behind(normed[rows - part :], ("seqa", "seqb"), whole + 1))
    head = normed[: rows - part]
    if whole > 0:
        head = from_behind(head, ("seqa", "seqb"), whole)
    pieces.append(head)
    return jnp.concatenate(pieces, axis=0)


def one_layer(hidden_state, tap_prev, tap_now, bias, mixing, dilation_step):
    normed = norm_rows(hidden_state)
    earlier = block_prior(normed, dilation_step)
    dim = hidden_state.shape[1]
    pre = bias[None, :] + jnp.dot(
        earlier,
        lax.all_gather(tap_prev, "seqa", axis=0, tiled=True),
        preferred_element_type=jnp.float32,
    )
    pre = pre + jnp.dot(
        normed,
        lax.all_gather(tap_now, "seqa", axis=0, tiled=True),
        preferred_element_type=jnp.float32,
    )
    hidden = (pre[:, :dim] * jax.nn.sigmoid(pre[:, dim:])).astype(jnp.bfloat16)
    return hidden_state + jnp.dot(
        hidden,
        lax.all_gather(mixing, "seqa", axis=1, tiled=True),
        preferred_element_type=jnp.float32,
    )


def plain_local(sequence_input, w_prev, w_now, conv_bias, w_mix):
    state = sequence_input.astype(jnp.float32)
    for layer, step in enumerate(DILATIONS):
        state = one_layer(
            state, w_prev[layer], w_now[layer], conv_bias[layer], w_mix[layer], step
        )
    return state.astype(jnp.bfloat16)


def flip(value, bit):
    return value + bit - 2 * bit * ((value // bit) % 2)


def block_kernel(
    na, nb, chunk,
    x_hbm, wp_hbm, wn_hbm, bias_ref, wm_hbm,
    out_ref,
    w, xin, xs, state, u0, u1, u2, h1, h2, pre, osend, oin,
    load_sem, x_sem, own_sem, send, recv, halo_send, halo_recv, hello,
):
    layers, dim = wp_hbm.shape[0], x_hbm.shape[1]
    wide = 2 * dim
    shard = wp_hbm.shape[1]
    rows = x_hbm.shape[0]
    n = na * nb
    part = DILATIONS[0]
    a, b = lax.axis_index("seqa"), lax.axis_index("seqb")
    me = a * nb + b
    a1, a2 = flip(a, 1), flip(a, 2)
    b1, b2 = flip(b, 1), flip(b, 2)
    tiles = shard // TILE
    zs = tiles // 5
    ys = tiles // 2 - zs
    yb, zb = b % 2, b // 2 % 2
    shares = [(ys, zs), (ys - 2, zs), (ys - 1, zs)]

    def at(index):
        return (index // nb, index % nb)

    hop = DILATIONS[2] // rows
    half, q = b // hop, b % hop
    other = 1 - half
    pair = (a, (b + hop) % nb)
    follow_a, follow_q = (a + 1) % na, (q + 1) % hop
    wrap = (q + 1) // hop
    next_b = half * hop + follow_q

    loads = []
    for l in range(layers):
        loads.append([
            pltpu.make_async_copy(wp_hbm.at[l], w.at[l, a, :, pl.ds(0, wide)], load_sem.at[l, 0]),
            pltpu.make_async_copy(wn_hbm.at[l], w.at[l, a, :, pl.ds(wide, wide)], load_sem.at[l, 1]),
            pltpu.make_async_copy(wm_hbm.at[l], w.at[l, a, :, pl.ds(2 * wide, dim)], load_sem.at[l, 2]),
        ])
    for c in loads[0]:
        c.start()
    x_load = pltpu.make_async_copy(x_hbm, xin, x_sem)
    x_load.start()
    for l in range(1, layers):
        for c in loads[l]:
            c.start()
    barrier = pltpu.get_barrier_semaphore()
    first, last_one = b == 0, b == nb - 1
    sends_next = jnp.logical_and(me + 1 < n, (b + 1) % nb < hop)
    sends_back = jnp.logical_and(b >= hop - 1, b < 2 * hop - 1)
    takes_next = jnp.logical_and(half == 0, me > 0)
    z = b // 2
    inner = jnp.logical_and(z > 0, z < nb // 2 - 1)
    beside = (a, (b + nb - 2 + 4 * (z % 2)) % nb)

    def greet(sem, more):
        count = 4
        for dev in ((a1, b), (a2, b), (a, b1), (a, b2)):
            pl.semaphore_signal(sem, inc=1, device_id=dev, device_id_type=MESH_ID)
        for to, dev, come in [(inner, beside, inner)] + more:
            @pl.when(to)
            def _(dev=dev):
                pl.semaphore_signal(sem, inc=1, device_id=dev, device_id_type=MESH_ID)

            count = count + come.astype(jnp.int32)
        pl.semaphore_wait(sem, count)

    up, down = a + 1 < na, a > 0
    before = (a + na - 1) % na
    last_b = half * hop + (q + hop - 1) % hop
    greet(barrier, [
        (jnp.logical_and(first, down), (before, nb - 1), jnp.logical_and(last_one, up)),
        (half == 0, (a, (b + hop - 1) % nb), sends_back),
        (half == 0, pair, half == 1),
        (q == 0, (a, last_b), wrap == 1),
        (jnp.logical_and(q == 0, down), (before, last_b), jnp.logical_and(wrap == 1, up)),
    ])

    def move(l, k, owner, start, size, dev):
        ref = w.at[l, owner, pl.ds(pl.multiple_of(start * TILE, TILE), size * TILE)]
        return pltpu.make_async_remote_copy(
            src_ref=ref, dst_ref=ref, send_sem=send.at[l, k], recv_sem=recv.at[l, k],
            device_id=dev, device_id_type=MESH_ID,
        )

    core, across, ynear, znear = (a1, b), (a2, b), (a, b1), (a, b2)
    moves, orders, lasts = [], [], []
    for l, (y, z) in enumerate(shares):
        rest = tiles - 2 * (y + z)
        own = (yb * y, 2 * y + zb * z, 2 * (y + z))
        theirs = ((1 - yb) * y, 2 * y + (1 - zb) * z)
        sizes = (y, z, rest)
        order = [(1, i) for i in range(z)] + [(0, i) for i in range(y)] + [(2, i) for i in range(rest)]
        pieces = len(order)
        here = [move(l, k, a, own[f] + i, 1, across) for k, (f, i) in enumerate(order)]
        relays = {}
        for k, (f, i) in enumerate(order):
            if f < 2:
                relays[k] = len(here)
                here.append(move(l, len(here), a2, own[f] + i, 1, (ynear, znear)[f]))
        last = len(here)
        here.append(move(l, last, a, 0, tiles, core))
        for f in range(3):
            if sizes[f]:
                here.append(move(l, len(here), a2, own[f], sizes[f], core))
        for f in range(2):
            here.append(move(l, len(here), a2, theirs[f], sizes[f], core))
        moves.append(here)
        orders.append((order, sizes, relays))
        lasts.append(last)

    held = 0

    def start_weights(l, hold=0):
        for k in range(len(orders[l][0]) - hold):
            moves[l][k].start()
        moves[l][lasts[l]].start()

    def relay(l, k):
        order, sizes, relays = orders[l]
        moves[l][k].wait_recv()
        f, i = order[k]
        if k in relays:
            moves[l][relays[k]].start()
        if i == sizes[f] - 1:
            moves[l][lasts[l] + 1 + f].start()

    def gather(l, f):
        order, sizes, relays = orders[l]
        for k in relays:
            if order[k][0] == f:
                moves[l][relays[k]].wait_recv()
        moves[l][len(moves[l]) - 2 + f].start()

    def finish(l):
        for k in range(lasts[l], len(moves[l])):
            moves[l][k].wait_recv()

    def halo(src, dst, slot, dev):
        return pltpu.make_async_remote_copy(
            src_ref=src, dst_ref=dst, send_sem=halo_send.at[slot], recv_sem=halo_recv.at[slot],
            device_id=dev, device_id_type=MESH_ID,
        )

    pair_low = halo(xin.at[pl.ds(part, rows - part)], xs.at[0], 0, pair)
    pair_high = halo(xin.at[pl.ds(0, chunk)], xs.at[1, pl.ds(part, chunk)], 0, pair)
    tail_src = xin.at[pl.ds(rows - part, part)]
    tail_next = halo(tail_src, xs.at[0, pl.ds(0, part)], 1, at((me + 1) % n))
    tail_back = halo(tail_src, xs.at[1, pl.ds(0, part)], 2, at((me + n - hop + 1) % n))
    def second(s):
        to = s + wrap
        slot = to % 2
        dev = ((a + to // 2) % na, next_b)
        return pltpu.make_async_remote_copy(
            src_ref=u1.at[s], dst_ref=h1.at[slot], send_sem=halo_send.at[3 + slot],
            recv_sem=halo_recv.at[3 + slot], device_id=dev, device_id_type=MESH_ID,
        ), a + to // 2 < na

    third = halo(u2.at[1], h2.at[0], 5, (follow_a, b))
    back = halo(osend, oin, 6, pair)

    def send_pair():
        @pl.when(half == 0)
        def _():
            pair_low.start()

        @pl.when(half == 1)
        def _():
            pair_high.start()

    near_cut = (b // 2) % 2 != half
    own_low = pltpu.make_async_copy(xin.at[pl.ds(0, chunk)], xs.at[0, pl.ds(part, chunk)], own_sem)
    own_high = pltpu.make_async_copy(xin.at[pl.ds(part, rows - part)], xs.at[1], own_sem)

    for c in loads[0]:
        c.wait()
    start_weights(0)
    x_load.wait()

    greet(hello, [])
    @pl.when(sends_next)
    def _():
        tail_next.start()

    @pl.when(sends_back)
    def _():
        tail_back.start()

    pl.when(near_cut)(send_pair)

    @pl.when(half == 0)
    def _():
        own_low.start()
        own_low.wait()

    @pl.when(half == 1)
    def _():
        own_high.start()
        own_high.wait()

    for l in range(1, layers):
        for c in loads[l]:
            c.wait()
        start_weights(l, held if l == layers - 1 else 0)
    @pl.when(me == 0)
    def _():
        xs[0, pl.ds(0, part), :] = jnp.zeros((part, dim), xs.dtype)

    @pl.when(jnp.logical_and(a == 0, q == 0))
    def _():
        h1[0] = jnp.zeros(h1.shape[1:], h1.dtype)

    @pl.when(a == 0)
    def _():
        h2[0] = jnp.zeros(h2.shape[1:], h2.dtype)

    def enter(s):
        block = xs[s].astype(jnp.float32)
        u0[s] = norm_rows(block)
        state[s] = block[part:]

    relay(0, 0)
    relay(0, 1)
    pl.when(jnp.logical_not(near_cut))(send_pair)
    for k in range(2, 5):
        relay(0, k)
    gather(0, 1)
    relay(1, 0)
    gather(0, 0)

    @pl.when(takes_next)
    def _():
        tail_next.wait_recv()

    enter(half)
    relay(1, 1)
    finish(0)

    def tap(l, lo):
        return w[l, :, :, lo : lo + wide].reshape(na * shard, wide)

    def now_part(l, now, s):
        pre[s] = bias_ref[l : l + 1, :] + jnp.dot(
            now, tap(l, wide), preferred_element_type=jnp.float32
        )

    def rest_part(l, earlier, s):
        total = pre[s] + jnp.dot(earlier, tap(l, 0), preferred_element_type=jnp.float32)
        hidden = (total[:, :dim] * jax.nn.sigmoid(total[:, dim:])).astype(jnp.bfloat16)
        mix = w[l, :, :, 2 * wide :].reshape(na * shard, dim)
        return state[s] + lax.dot_general(
            hidden, mix, (((1,), (1,)), ((), ())), preferred_element_type=jnp.float32
        )

    for c, s in enumerate((half, other)):
        if c == 1:
            @pl.when(half == 1)
            def _():
                pair_low.wait_recv()

            @pl.when(half == 0)
            def _():
                pair_high.wait_recv()
                tail_back.wait_recv()

            enter(s)
        now_part(0, u0[s, pl.ds(part, chunk), :], s)
        relay(1, 2 + c)
        new = rest_part(0, u0[s, pl.ds(0, chunk), :], s)
        state[s] = new
        u1[s] = norm_rows(new)
        copy, there = second(s)
        pl.when(there)(copy.start)
    for k in range(4, len(orders[1][0])):
        relay(1, k)
    gather(1, 1)
    gather(1, 0)
    finish(1)
    for s in (half, other):
        now_part(1, u1[s], s)
    for c, s in enumerate((half, other)):
        @pl.when(jnp.logical_or(me % nb % hop + s > 0, a > 0))
        def _(s=s):
            halo(u1.at[s], h1.at[s], 3 + s, pair).wait_recv()

        relay(2, c)
        new = rest_part(1, h1[s], s)
        state[s] = new
        normed = norm_rows(new)
        u2[s] = normed

        @pl.when(s == 0)
        def _(normed=normed):
            h2[1] = normed

        @pl.when(jnp.logical_and(s == 1, a + 1 < na))
        def _():
            third.start()

    for k in range(len(orders[2][0]) - held, len(orders[2][0])):
        moves[2][k].start()
    for k in range(2, len(orders[2][0])):
        relay(2, k)
    gather(2, 1)
    gather(2, 0)
    finish(2)
    for c, s in enumerate((other, half)):
        now_part(2, u2[s], s)

        @pl.when(jnp.logical_and(s == 0, a > 0))
        def _():
            third.wait_recv()

        new = rest_part(2, h2[s], s).astype(out_ref.dtype)
        if c == 0:
            osend[...] = new
            back.start()
        else:
            out_ref[pl.ds(pl.multiple_of(half * chunk, chunk), chunk), :] = new
    back.wait_recv()
    out_ref[pl.ds(pl.multiple_of(other * chunk, chunk), chunk), :] = oin[...]

    for l in range(layers):
        for m in moves[l]:
            m.wait_send()
    back.wait_send()
    for s in range(2):
        copy, there = second(s)
        pl.when(there)(copy.wait_send)
    pl.when(a + 1 < na)(third.wait_send)
    pl.when(sends_next)(tail_next.wait_send)
    pl.when(sends_back)(tail_back.wait_send)
    pl.when(half == 0)(pair_low.wait_send)
    pl.when(half == 1)(pair_high.wait_send)


def kernel_local(na, nb, sequence_input, w_prev, w_now, conv_bias, w_mix):
    rows, dim = sequence_input.shape
    layers, shard, wide = w_prev.shape
    chunk = rows // 2
    part = DILATIONS[0]
    bf16, f32 = jnp.bfloat16, jnp.float32
    halos = 7
    copies = shard // TILE + 6
    anywhere = pl.BlockSpec(memory_space=pl.ANY)
    vmem = pl.BlockSpec(memory_space=pltpu.VMEM)
    return pl.pallas_call(
        functools.partial(block_kernel, na, nb, chunk),
        out_shape=jax.ShapeDtypeStruct((rows, dim), bf16),
        in_specs=[anywhere, anywhere, anywhere, vmem, anywhere],
        out_specs=vmem,
        scratch_shapes=[
            pltpu.VMEM((layers, na, shard, 2 * wide + dim), bf16),
            pltpu.VMEM((rows, dim), bf16),
            pltpu.VMEM((2, part + chunk, dim), bf16),
            pltpu.VMEM((2, chunk, dim), f32),
            pltpu.VMEM((2, part + chunk, dim), bf16),
            pltpu.VMEM((2, chunk, dim), bf16),
            pltpu.VMEM((2, chunk, dim), bf16),
            pltpu.VMEM((2, chunk, dim), bf16),
            pltpu.VMEM((2, chunk, dim), bf16),
            pltpu.VMEM((2, chunk, wide), f32),
            pltpu.VMEM((chunk, dim), bf16),
            pltpu.VMEM((chunk, dim), bf16),
            pltpu.SemaphoreType.DMA((layers, 3)),
            pltpu.SemaphoreType.DMA,
            pltpu.SemaphoreType.DMA,
            pltpu.SemaphoreType.DMA((layers, copies)),
            pltpu.SemaphoreType.DMA((layers, copies)),
            pltpu.SemaphoreType.DMA((halos,)),
            pltpu.SemaphoreType.DMA((halos,)),
            pltpu.SemaphoreType.REGULAR,
        ],
        compiler_params=pltpu.CompilerParams(
            collective_id=0, has_side_effects=True, vmem_limit_bytes=56 * 2**20
        ),
    )(sequence_input, w_prev, w_now, conv_bias, jnp.swapaxes(w_mix, 1, 2))


def local(na, nb, sequence_input, w_prev, w_now, conv_bias, w_mix):
    rows = sequence_input.shape[0]
    shard = w_prev.shape[1]
    fits = (
        na == 4
        and nb % GROUP == 0
        and shard % TILE == 0
        and shard % (2 * TILE) == 0
        and shard >= 5 * TILE
        and rows % (4 * TILE) == 0
        and rows == 4 * DILATIONS[0]
        and DILATIONS[1] == rows
        and 2 * DILATIONS[2] == nb * rows
    )
    body = functools.partial(kernel_local, na, nb) if fits else plain_local
    return body(sequence_input, w_prev, w_now, conv_bias, w_mix)


def solution(mesh):
    return jax.shard_map(
        functools.partial(local, mesh.shape["seqa"], mesh.shape["seqb"]),
        mesh=mesh,
        in_specs=(
            P(("seqa", "seqb"), None),
            P(None, "seqa", None),
            P(None, "seqa", None),
            P(),
            P(None, None, "seqa"),
        ),
        out_specs=P(("seqa", "seqb"), None),
        check_vma=False,
    )
```

```python
import functools

import jax
import jax.numpy as jnp
from jax import lax
from jax.experimental import pallas as pl
from jax.experimental.pallas import tpu as pltpu
from jax.sharding import PartitionSpec as P

DILATIONS = (128, 512, 2048)
EPS = 1e-06
TILE = 16
GROUP = 4
MESH_ID = pl.DeviceIdType.MESH


def from_behind(value, axis, by):
    peers = lax.axis_size(axis)
    pairs = [(i, i + by) for i in range(peers) if 0 <= i + by < peers]
    return lax.ppermute(value, axis, pairs)


def norm_rows(values):
    scale = lax.rsqrt(jnp.mean(values * values, axis=1, keepdims=True) + EPS)
    return (values * scale).astype(jnp.bfloat16)


def block_prior(normed, dilation_step):
    rows = normed.shape[0]
    whole = dilation_step // rows
    part = dilation_step % rows
    pieces = []
    if part > 0:
        pieces.append(from_behind(normed[rows - part :], ("seqa", "seqb"), whole + 1))
    head = normed[: rows - part]
    if whole > 0:
        head = from_behind(head, ("seqa", "seqb"), whole)
    pieces.append(head)
    return jnp.concatenate(pieces, axis=0)


def one_layer(hidden_state, tap_prev, tap_now, bias, mixing, dilation_step):
    normed = norm_rows(hidden_state)
    earlier = block_prior(normed, dilation_step)
    dim = hidden_state.shape[1]
    pre = bias[None, :] + jnp.dot(
        earlier,
        lax.all_gather(tap_prev, "seqa", axis=0, tiled=True),
        preferred_element_type=jnp.float32,
    )
    pre = pre + jnp.dot(
        normed,
        lax.all_gather(tap_now, "seqa", axis=0, tiled=True),
        preferred_element_type=jnp.float32,
    )
    hidden = (pre[:, :dim] * jax.nn.sigmoid(pre[:, dim:])).astype(jnp.bfloat16)
    return hidden_state + jnp.dot(
        hidden,
        lax.all_gather(mixing, "seqa", axis=1, tiled=True),
        preferred_element_type=jnp.float32,
    )


def plain_local(sequence_input, w_prev, w_now, conv_bias, w_mix):
    state = sequence_input.astype(jnp.float32)
    for layer, step in enumerate(DILATIONS):
        state = one_layer(
            state, w_prev[layer], w_now[layer], conv_bias[layer], w_mix[layer], step
        )
    return state.astype(jnp.bfloat16)


def flip(value, bit):
    return value + bit - 2 * bit * ((value // bit) % 2)


def block_kernel(
    na, nb, part, edge,
    x_hbm, wp_hbm, wn_hbm, bias_ref, wm_hbm,
    out_hbm,
    w, xin, xt, xp, state1, state2, u0, h0, u1, h1, u2, h2, pre, oback, ohome,
    load_sem, x_sem, out_sem, send, recv, halo_send, halo_recv, hello,
):
    layers, dim = wp_hbm.shape[0], x_hbm.shape[1]
    wide = 2 * dim
    shard = wp_hbm.shape[1]
    rows = x_hbm.shape[0]
    n = na * nb
    tail = DILATIONS[0]
    window = edge + tail
    lead_rows = edge + part
    f32, bf16 = jnp.float32, jnp.bfloat16
    a, b = lax.axis_index("seqa"), lax.axis_index("seqb")
    me = a * nb + b
    a1, a2 = flip(a, 1), flip(a, 2)
    b1, b2 = flip(b, 1), flip(b, 2)
    tiles = shard // TILE
    zs = tiles // 5
    ys = tiles // 2 - zs
    yb, zb = b % 2, b // 2 % 2
    shares = [(ys, zs), (ys - 2, zs), (ys - 1, zs)]

    def at(index):
        return (index // nb, index % nb)

    hop = DILATIONS[2] // rows
    half, q = b // hop, b % hop
    other = 1 - half
    pair = (a, (b + hop) % nb)
    wrap = (q + 1) // hop
    next_b = half * hop + (q + 1) % hop
    last_b = half * hop + (q + hop - 1) % hop
    after_a, before_a = (a + 1) % na, (a + na - 1) % na
    up, down = a + 1 < na, a > 0
    has_next, has_last = me + 1 < n, me > 0
    has_far, had_far = me + hop < n, me >= hop
    lead = jnp.where(q == 0, other, half)

    def place1(s):
        return pl.multiple_of(jnp.where(s == lead, 0, lead_rows), TILE)

    def place2(s):
        return pl.multiple_of(jnp.where(s == half, 0, lead_rows), TILE)

    loads = []
    for l in range(layers):
        loads.append([
            pltpu.make_async_copy(wp_hbm.at[l], w.at[l, a, :, pl.ds(0, wide)], load_sem.at[l, 0]),
            pltpu.make_async_copy(wn_hbm.at[l], w.at[l, a, :, pl.ds(wide, wide)], load_sem.at[l, 1]),
            pltpu.make_async_copy(wm_hbm.at[l], w.at[l, a, :, pl.ds(2 * wide, dim)], load_sem.at[l, 2]),
        ])
    for c in loads[0]:
        c.start()
    x_load = pltpu.make_async_copy(x_hbm, xin, x_sem)
    x_load.start()
    for l in range(1, layers):
        for c in loads[l]:
            c.start()

    z = b // 2
    inner = jnp.logical_and(z > 0, z < nb // 2 - 1)
    beside = (a, (b + nb - 2 + 4 * (z % 2)) % nb)

    def greet(sem, more):
        count = 4
        for dev in ((a1, b), (a2, b), (a, b1), (a, b2)):
            pl.semaphore_signal(sem, inc=1, device_id=dev, device_id_type=MESH_ID)
        for to, dev, come in [(inner, beside, inner)] + more:
            @pl.when(to)
            def _(dev=dev):
                pl.semaphore_signal(sem, inc=1, device_id=dev, device_id_type=MESH_ID)

            count = count + come.astype(jnp.int32)
        pl.semaphore_wait(sem, count)

    both = jnp.logical_and
    greet(pltpu.get_barrier_semaphore(), [
        (both(b == 0, down), (before_a, nb - 1), both(b == nb - 1, up)),
        (half == 0, pair, half == 1),
        (both(half == 0, down), (before_a, (b + hop) % nb), both(half == 1, up)),
        (q == 0, (a, last_b), wrap == 1),
        (both(q == 0, down), (before_a, last_b), both(wrap == 1, up)),
    ])

    def move(l, k, owner, start, size, dev):
        ref = w.at[l, owner, pl.ds(pl.multiple_of(start * TILE, TILE), size * TILE)]
        return pltpu.make_async_remote_copy(
            src_ref=ref, dst_ref=ref, send_sem=send.at[l, k], recv_sem=recv.at[l, k],
            device_id=dev, device_id_type=MESH_ID,
        )

    core, across, ynear, znear = (a1, b), (a2, b), (a, b1), (a, b2)
    moves, orders, lasts = [], [], []
    for l, (y, z) in enumerate(shares):
        rest = tiles - 2 * (y + z)
        own = (yb * y, 2 * y + zb * z, 2 * (y + z))
        theirs = ((1 - yb) * y, 2 * y + (1 - zb) * z)
        sizes = (y, z, rest)
        order = [(1, i) for i in range(z)] + [(0, i) for i in range(y)] + [(2, i) for i in range(rest)]
        pieces = len(order)
        here = [move(l, k, a, own[f] + i, 1, across) for k, (f, i) in enumerate(order)]
        relays = {}
        for k, (f, i) in enumerate(order):
            if f < 2:
                relays[k] = len(here)
                here.append(move(l, len(here), a2, own[f] + i, 1, (ynear, znear)[f]))
        last = len(here)
        here.append(move(l, last, a, 0, tiles, core))
        for f in range(3):
            if sizes[f]:
                here.append(move(l, len(here), a2, own[f], sizes[f], core))
        for f in range(2):
            here.append(move(l, len(here), a2, theirs[f], sizes[f], core))
        moves.append(here)
        orders.append((order, sizes, relays))
        lasts.append(last)

    def start_weights(l):
        for k in range(len(orders[l][0])):
            moves[l][k].start()
        moves[l][lasts[l]].start()

    def relay(l, k):
        order, sizes, relays = orders[l]
        moves[l][k].wait_recv()
        f, i = order[k]
        if k in relays:
            moves[l][relays[k]].start()
        if i == sizes[f] - 1:
            moves[l][lasts[l] + 1 + f].start()

    def gather(l, f):
        order, sizes, relays = orders[l]
        for k in relays:
            if order[k][0] == f:
                moves[l][relays[k]].wait_recv()
        moves[l][len(moves[l]) - 2 + f].start()

    def finish(l):
        for k in range(lasts[l], len(moves[l])):
            moves[l][k].wait_recv()

    def halo(src, dst, slot, dev):
        return pltpu.make_async_remote_copy(
            src_ref=src, dst_ref=dst, send_sem=halo_send.at[slot], recv_sem=halo_recv.at[slot],
            device_id=dev, device_id_type=MESH_ID,
        )

    mine = pl.ds(edge, part)
    x_next = halo(xin.at[pl.ds(rows - tail, tail)], xt, 0, at((me + 1) % n))
    x_pair = halo(xin.at[pl.ds(pl.multiple_of(other * edge, TILE), window)], xp, 1, pair)
    second_home = halo(u1.at[mine], h1.at[mine], 2, at((me + 1) % n))

    def second(s):
        to = s + wrap
        slot = to % 2
        return halo(
            u1.at[pl.ds(place1(s), edge)], h1.at[pl.ds(place1_at_next(slot), edge)],
            3 + slot, ((a + to // 2) % na, next_b),
        ), a + to // 2 < na

    def place1_at_next(slot):
        first = jnp.where(wrap == 1, other, half)
        return pl.multiple_of(jnp.where(slot == first, 0, lead_rows), TILE)

    third_home = halo(u2.at[mine], h2.at[mine], 5, at((me + hop) % n))
    third = halo(u2.at[pl.ds(place2(1), edge)], h2.at[pl.ds(place2(0), edge)], 6, (after_a, b))
    edge_rows = pl.ds(pl.multiple_of(part + half * edge, TILE), edge)
    back = halo(oback, out_hbm.at[edge_rows], 7, pair)
    near_cut = (b // 2) % 2 != half

    for c in loads[0]:
        c.wait()
    start_weights(0)
    x_load.wait()
    greet(hello, [])
    pl.when(has_next)(x_next.start)
    pl.when(near_cut)(x_pair.start)
    for l in range(1, layers):
        for c in loads[l]:
            c.wait()
        start_weights(l)

    @pl.when(me == 0)
    def _():
        xt[...] = jnp.zeros(xt.shape, xt.dtype)
        h1[mine] = jnp.zeros((part, dim), h1.dtype)

    @pl.when(both(a == 0, q == 0))
    def _():
        h1[pl.ds(place1(0), edge)] = jnp.zeros((edge, dim), h1.dtype)

    @pl.when(a == 0)
    def _():
        h2[pl.ds(place2(0), edge)] = jnp.zeros((edge, dim), h2.dtype)

    @pl.when(jnp.logical_not(had_far))
    def _():
        h2[mine] = jnp.zeros((part, dim), h2.dtype)

    def enter(ref, start, lo):
        normed = norm_rows(ref[pl.ds(start, window)].astype(f32))
        h0[lo : lo + edge] = normed[:edge]
        u0[lo : lo + edge] = normed[tail:]

    def tap(l, lo):
        return w[l, :, :, lo : lo + wide].reshape(na * shard, wide)

    front, rear = (0, lead_rows), (lead_rows, edge)

    def now_part(l, now, span):
        lo, size = span
        pre[lo : lo + size] = bias_ref[l : l + 1, :] + jnp.dot(
            now[lo : lo + size], tap(l, wide), preferred_element_type=f32
        )

    def rest_part(l, earlier, span):
        lo, size = span
        total = pre[lo : lo + size] + jnp.dot(
            earlier[lo : lo + size], tap(l, 0), preferred_element_type=f32
        )
        hidden = (total[:, :dim] * jax.nn.sigmoid(total[:, dim:])).astype(bf16)
        mix = w[l, :, :, 2 * wide :].reshape(na * shard, dim)
        return lax.dot_general(hidden, mix, (((1,), (1,)), ((), ())), preferred_element_type=f32)

    enter(xin, pl.multiple_of(half * edge, TILE), 0)
    u0[mine] = norm_rows(xin[:part].astype(f32))
    relay(0, 0)
    relay(0, 1)
    pl.when(jnp.logical_not(near_cut))(x_pair.start)
    for k in range(2, len(orders[0][0])):
        relay(0, k)
    gather(0, 1)
    relay(1, 0)
    gather(0, 0)
    pl.when(has_last)(x_next.wait_recv)
    h0[mine] = norm_rows(xt[...].astype(f32))
    relay(1, 1)
    finish(0)

    def leave1(new, spot):
        state1[spot] = new
        u1[spot] = norm_rows(new)

    now_part(0, u0, front)
    relay(1, 2)
    grown = rest_part(0, h0, front)
    own_start = pl.multiple_of(tail + half * edge, TILE)
    leave1(xin[pl.ds(own_start, edge)].astype(f32) + grown[:edge], pl.ds(place1(half), edge))
    copy, there = second(half)
    pl.when(there)(copy.start)
    leave1(xin[:part].astype(f32) + grown[edge:], mine)
    pl.when(has_next)(second_home.start)
    x_pair.wait_recv()
    enter(xp, 0, lead_rows)
    now_part(0, u0, rear)
    relay(1, 3)
    grown = rest_part(0, h0, rear)
    leave1(xp[tail:].astype(f32) + grown, pl.ds(place1(other), edge))
    copy, there = second(other)
    pl.when(there)(copy.start)
    for k in range(4, len(orders[1][0])):
        relay(1, k)
    gather(1, 1)
    gather(1, 0)
    finish(1)
    now_part(1, u1, front)
    now_part(1, u1, rear)
    relay(2, 0)

    def takes(s):
        @pl.when(jnp.logical_or(q + s > 0, down))
        def _():
            spot = pl.ds(place1(s), edge)
            halo(u1.at[spot], h1.at[spot], 3 + s, pair).wait_recv()

    def leave2(new, spot):
        normed = norm_rows(new)
        state2[spot] = new
        u2[spot] = normed
        return normed

    def leave2_edge(new, s):
        normed = leave2(new, pl.ds(place2(s), edge))

        @pl.when(s == 0)
        def _():
            h2[pl.ds(place2(1), edge)] = normed

        @pl.when(both(s == 1, up))
        def _():
            third.start()

    takes(lead)
    pl.when(has_last)(second_home.wait_recv)
    new = state1[:lead_rows] + rest_part(1, h1, front)
    leave2(new[edge:], mine)
    pl.when(has_far)(third_home.start)
    leave2_edge(new[:edge], lead)
    relay(2, 1)
    relay(2, 2)
    takes(1 - lead)
    leave2_edge(state1[lead_rows:] + rest_part(1, h1, rear), 1 - lead)
    for k in range(3, len(orders[2][0])):
        relay(2, k)
    gather(2, 1)
    gather(2, 0)
    finish(2)

    def takes_third(s):
        @pl.when(both(s == 0, down))
        def _():
            third.wait_recv()

    now_part(2, u2, rear)
    takes_third(other)
    oback[...] = (state2[lead_rows:] + rest_part(2, h2, rear)).astype(bf16)
    back.start()
    now_part(2, u2, front)
    takes_third(half)
    pl.when(had_far)(third_home.wait_recv)
    ohome[...] = (state2[:lead_rows] + rest_part(2, h2, front)).astype(bf16)
    outs = [
        pltpu.make_async_copy(ohome.at[pl.ds(0, edge)], out_hbm.at[edge_rows], out_sem.at[0]),
        pltpu.make_async_copy(ohome.at[mine], out_hbm.at[pl.ds(0, part)], out_sem.at[1]),
    ]
    for c in outs:
        c.start()
    for l in range(layers):
        for m in moves[l]:
            m.wait_send()
    for s in range(2):
        copy, there = second(s)
        pl.when(there)(copy.wait_send)
    pl.when(has_next)(second_home.wait_send)
    pl.when(has_next)(x_next.wait_send)
    pl.when(has_far)(third_home.wait_send)
    pl.when(up)(third.wait_send)
    x_pair.wait_send()
    for c in outs:
        c.wait()
    back.wait_send()
    back.wait_recv()


def kernel_local(na, nb, sequence_input, w_prev, w_now, conv_bias, w_mix):
    rows, dim = sequence_input.shape
    layers, shard, wide = w_prev.shape
    tail = DILATIONS[0]
    part = tail
    edge = (rows - part) // 2
    bf16, f32 = jnp.bfloat16, jnp.float32
    halos, copies = 8, shard // TILE + 6
    anywhere = pl.BlockSpec(memory_space=pl.ANY)
    vmem = pl.BlockSpec(memory_space=pltpu.VMEM)
    block = (rows, dim)
    return pl.pallas_call(
        functools.partial(block_kernel, na, nb, part, edge),
        out_shape=jax.ShapeDtypeStruct((rows, dim), bf16),
        in_specs=[anywhere, anywhere, anywhere, vmem, anywhere],
        out_specs=anywhere,
        scratch_shapes=[
            pltpu.VMEM((layers, na, shard, 2 * wide + dim), bf16),
            pltpu.VMEM(block, bf16),
            pltpu.VMEM((tail, dim), bf16),
            pltpu.VMEM((edge + tail, dim), bf16),
            pltpu.VMEM(block, f32),
            pltpu.VMEM(block, f32),
            pltpu.VMEM(block, bf16),
            pltpu.VMEM(block, bf16),
            pltpu.VMEM(block, bf16),
            pltpu.VMEM(block, bf16),
            pltpu.VMEM(block, bf16),
            pltpu.VMEM(block, bf16),
            pltpu.VMEM((rows, wide), f32),
            pltpu.VMEM((edge, dim), bf16),
            pltpu.VMEM((edge + part, dim), bf16),
            pltpu.SemaphoreType.DMA((layers, 3)),
            pltpu.SemaphoreType.DMA,
            pltpu.SemaphoreType.DMA((2,)),
            pltpu.SemaphoreType.DMA((layers, copies)),
            pltpu.SemaphoreType.DMA((layers, copies)),
            pltpu.SemaphoreType.DMA((halos,)),
            pltpu.SemaphoreType.DMA((halos,)),
            pltpu.SemaphoreType.REGULAR,
        ],
        compiler_params=pltpu.CompilerParams(
            collective_id=0, has_side_effects=True, vmem_limit_bytes=56 * 2**20
        ),
    )(sequence_input, w_prev, w_now, conv_bias, jnp.swapaxes(w_mix, 1, 2))


def local(na, nb, sequence_input, w_prev, w_now, conv_bias, w_mix):
    rows = sequence_input.shape[0]
    shard = w_prev.shape[1]
    fits = (
        na == 4
        and nb % GROUP == 0
        and shard % TILE == 0
        and shard % (2 * TILE) == 0
        and shard >= 5 * TILE
        and rows % (4 * TILE) == 0
        and rows == 4 * DILATIONS[0]
        and DILATIONS[1] == rows
        and 2 * DILATIONS[2] == nb * rows
    )
    body = functools.partial(kernel_local, na, nb) if fits else plain_local
    return body(sequence_input, w_prev, w_now, conv_bias, w_mix)


def solution(mesh):
    return jax.shard_map(
        functools.partial(local, mesh.shape["seqa"], mesh.shape["seqb"]),
        mesh=mesh,
        in_specs=(
            P(("seqa", "seqb"), None),
            P(None, "seqa", None),
            P(None, "seqa", None),
            P(),
            P(None, None, "seqa"),
        ),
        out_specs=P(("seqa", "seqb"), None),
        check_vma=False,
    )
```

```python
import functools

import jax
import jax.numpy as jnp
from jax import lax
from jax.experimental import pallas as pl
from jax.experimental.pallas import tpu as pltpu
from jax.sharding import PartitionSpec as P

DILATIONS = (128, 512, 2048)
EPS = 1e-06
TILE = 16
GROUP = 4
MESH_ID = pl.DeviceIdType.MESH


def from_behind(value, axis, by):
    peers = lax.axis_size(axis)
    pairs = [(i, i + by) for i in range(peers) if 0 <= i + by < peers]
    return lax.ppermute(value, axis, pairs)


def norm_rows(values):
    scale = lax.rsqrt(jnp.mean(values * values, axis=1, keepdims=True) + EPS)
    return (values * scale).astype(jnp.bfloat16)


def block_prior(normed, dilation_step):
    rows = normed.shape[0]
    whole = dilation_step // rows
    part = dilation_step % rows
    pieces = []
    if part > 0:
        pieces.append(from_behind(normed[rows - part :], ("seqa", "seqb"), whole + 1))
    head = normed[: rows - part]
    if whole > 0:
        head = from_behind(head, ("seqa", "seqb"), whole)
    pieces.append(head)
    return jnp.concatenate(pieces, axis=0)


def one_layer(hidden_state, tap_prev, tap_now, bias, mixing, dilation_step):
    normed = norm_rows(hidden_state)
    earlier = block_prior(normed, dilation_step)
    dim = hidden_state.shape[1]
    pre = bias[None, :] + jnp.dot(
        earlier,
        lax.all_gather(tap_prev, "seqa", axis=0, tiled=True),
        preferred_element_type=jnp.float32,
    )
    pre = pre + jnp.dot(
        normed,
        lax.all_gather(tap_now, "seqa", axis=0, tiled=True),
        preferred_element_type=jnp.float32,
    )
    hidden = (pre[:, :dim] * jax.nn.sigmoid(pre[:, dim:])).astype(jnp.bfloat16)
    return hidden_state + jnp.dot(
        hidden,
        lax.all_gather(mixing, "seqa", axis=1, tiled=True),
        preferred_element_type=jnp.float32,
    )


def plain_local(sequence_input, w_prev, w_now, conv_bias, w_mix):
    state = sequence_input.astype(jnp.float32)
    for layer, step in enumerate(DILATIONS):
        state = one_layer(
            state, w_prev[layer], w_now[layer], conv_bias[layer], w_mix[layer], step
        )
    return state.astype(jnp.bfloat16)


def flip(value, bit):
    return value + bit - 2 * bit * ((value // bit) % 2)


def block_kernel(
    na, nb, part, edge,
    x_hbm, wp_hbm, wn_hbm, bias_ref, wm_hbm,
    out_ref,
    w, xin, xt, xp, state1, state2, u0, h0, u1, h1, u2, h2, pre, oback,
    load_sem, x_sem, send, recv, halo_send, halo_recv, hello,
):
    layers, dim = wp_hbm.shape[0], x_hbm.shape[1]
    wide = 2 * dim
    shard = wp_hbm.shape[1]
    rows = x_hbm.shape[0]
    n = na * nb
    tail = DILATIONS[0]
    window = edge + tail
    lead_rows = edge + part
    f32, bf16 = jnp.float32, jnp.bfloat16
    a, b = lax.axis_index("seqa"), lax.axis_index("seqb")
    me = a * nb + b
    a1, a2 = flip(a, 1), flip(a, 2)
    b1, b2 = flip(b, 1), flip(b, 2)
    tiles = shard // TILE
    zs = tiles // 5
    ys = tiles // 2 - zs
    yb, zb = b % 2, b // 2 % 2
    shares = [(ys, zs), (ys - 2, zs), (ys - 1, zs - 1)]

    def at(index):
        return (index // nb, index % nb)

    hop = DILATIONS[2] // rows
    half, q = b // hop, b % hop
    other = 1 - half
    pair = (a, (b + hop) % nb)
    wrap = (q + 1) // hop
    next_b = half * hop + (q + 1) % hop
    last_b = half * hop + (q + hop - 1) % hop
    after_a, before_a = (a + 1) % na, (a + na - 1) % na
    up, down = a + 1 < na, a > 0
    has_next, has_last = me + 1 < n, me > 0
    has_far, had_far = me + hop < n, me >= hop
    lead = jnp.where(q == 0, other, half)

    def place1(s):
        return pl.multiple_of(jnp.where(s == lead, 0, lead_rows), TILE)

    def place2(s):
        return pl.multiple_of(jnp.where(s == half, 0, lead_rows), TILE)

    loads = []
    for l in range(layers):
        loads.append([
            pltpu.make_async_copy(wp_hbm.at[l], w.at[l, a, :, pl.ds(0, wide)], load_sem.at[l, 0]),
            pltpu.make_async_copy(wn_hbm.at[l], w.at[l, a, :, pl.ds(wide, wide)], load_sem.at[l, 1]),
            pltpu.make_async_copy(wm_hbm.at[l], w.at[l, a, :, pl.ds(2 * wide, dim)], load_sem.at[l, 2]),
        ])
    for c in loads[0]:
        c.start()
    x_load = pltpu.make_async_copy(x_hbm, xin, x_sem)
    x_load.start()
    for l in range(1, layers):
        for c in loads[l]:
            c.start()

    z = b // 2
    inner = jnp.logical_and(z > 0, z < nb // 2 - 1)
    beside = (a, (b + nb - 2 + 4 * (z % 2)) % nb)

    def greet(sem, more):
        count = 4
        for dev in ((a1, b), (a2, b), (a, b1), (a, b2)):
            pl.semaphore_signal(sem, inc=1, device_id=dev, device_id_type=MESH_ID)
        for to, dev, come in [(inner, beside, inner)] + more:
            @pl.when(to)
            def _(dev=dev):
                pl.semaphore_signal(sem, inc=1, device_id=dev, device_id_type=MESH_ID)

            count = count + come.astype(jnp.int32)
        pl.semaphore_wait(sem, count)

    both = jnp.logical_and
    greet(pltpu.get_barrier_semaphore(), [
        (both(b == 0, down), (before_a, nb - 1), both(b == nb - 1, up)),
        (half == 0, pair, half == 1),
        (both(half == 0, down), (before_a, (b + hop) % nb), both(half == 1, up)),
        (q == 0, (a, last_b), wrap == 1),
        (both(q == 0, down), (before_a, last_b), both(wrap == 1, up)),
    ])

    def move(l, k, owner, start, size, dev):
        ref = w.at[l, owner, pl.ds(pl.multiple_of(start * TILE, TILE), size * TILE)]
        return pltpu.make_async_remote_copy(
            src_ref=ref, dst_ref=ref, send_sem=send.at[l, k], recv_sem=recv.at[l, k],
            device_id=dev, device_id_type=MESH_ID,
        )

    core, across, ynear, znear = (a1, b), (a2, b), (a, b1), (a, b2)
    moves, orders, lasts = [], [], []
    for l, (y, z) in enumerate(shares):
        rest = tiles - 2 * (y + z)
        own = (yb * y, 2 * y + zb * z, 2 * (y + z))
        theirs = ((1 - yb) * y, 2 * y + (1 - zb) * z)
        sizes = (y, z, rest)
        order = [(1, i) for i in range(z)] + [(0, i) for i in range(y)] + [(2, i) for i in range(rest)]
        pieces = len(order)
        here = [move(l, k, a, own[f] + i, 1, across) for k, (f, i) in enumerate(order)]
        relays = {}
        for k, (f, i) in enumerate(order):
            if f < 2:
                relays[k] = len(here)
                here.append(move(l, len(here), a2, own[f] + i, 1, (ynear, znear)[f]))
        last = len(here)
        here.append(move(l, last, a, 0, tiles, core))
        for f in range(3):
            if sizes[f]:
                here.append(move(l, len(here), a2, own[f], sizes[f], core))
        for f in range(2):
            here.append(move(l, len(here), a2, theirs[f], sizes[f], core))
        moves.append(here)
        orders.append((order, sizes, relays))
        lasts.append(last)

    def start_weights(l):
        for k in range(len(orders[l][0])):
            moves[l][k].start()
        moves[l][lasts[l]].start()

    def relay(l, k):
        order, sizes, relays = orders[l]
        moves[l][k].wait_recv()
        f, i = order[k]
        if k in relays:
            moves[l][relays[k]].start()
        if i == sizes[f] - 1:
            moves[l][lasts[l] + 1 + f].start()

    def gather(l, f):
        order, sizes, relays = orders[l]
        for k in relays:
            if order[k][0] == f:
                moves[l][relays[k]].wait_recv()
        moves[l][len(moves[l]) - 2 + f].start()

    def finish(l):
        for k in range(lasts[l], len(moves[l])):
            moves[l][k].wait_recv()

    def halo(src, dst, slot, dev):
        return pltpu.make_async_remote_copy(
            src_ref=src, dst_ref=dst, send_sem=halo_send.at[slot], recv_sem=halo_recv.at[slot],
            device_id=dev, device_id_type=MESH_ID,
        )

    mine = pl.ds(edge, part)
    x_next = halo(xin.at[pl.ds(rows - tail, tail)], xt, 0, at((me + 1) % n))
    x_pair = halo(xin.at[pl.ds(pl.multiple_of(part - tail + other * edge, TILE), window)], xp, 1, pair)
    second_home = halo(u1.at[mine], h1.at[mine], 2, at((me + 1) % n))

    def second(s):
        to = s + wrap
        slot = to % 2
        return halo(
            u1.at[pl.ds(place1(s), edge)], h1.at[pl.ds(place1_at_next(slot), edge)],
            3 + slot, ((a + to // 2) % na, next_b),
        ), a + to // 2 < na

    def place1_at_next(slot):
        first = jnp.where(wrap == 1, other, half)
        return pl.multiple_of(jnp.where(slot == first, 0, lead_rows), TILE)

    third_home = halo(u2.at[mine], h2.at[mine], 5, at((me + hop) % n))
    third = halo(u2.at[pl.ds(place2(1), edge)], h2.at[pl.ds(place2(0), edge)], 6, (after_a, b))
    edge_rows = pl.ds(pl.multiple_of(part + half * edge, TILE), edge)
    back = halo(oback, out_ref.at[edge_rows], 7, pair)
    near_cut = (b // 2) % 2 != half

    for c in loads[0]:
        c.wait()
    start_weights(0)
    x_load.wait()
    greet(hello, [])
    pl.when(has_next)(x_next.start)
    pl.when(near_cut)(x_pair.start)
    for l in range(1, layers):
        for c in loads[l]:
            c.wait()
        start_weights(l)

    @pl.when(me == 0)
    def _():
        xt[...] = jnp.zeros(xt.shape, xt.dtype)
        h1[mine] = jnp.zeros((part, dim), h1.dtype)

    @pl.when(both(a == 0, q == 0))
    def _():
        h1[pl.ds(place1(0), edge)] = jnp.zeros((edge, dim), h1.dtype)

    @pl.when(a == 0)
    def _():
        h2[pl.ds(place2(0), edge)] = jnp.zeros((edge, dim), h2.dtype)

    @pl.when(jnp.logical_not(had_far))
    def _():
        h2[mine] = jnp.zeros((part, dim), h2.dtype)

    def enter(ref, start, lo):
        normed = norm_rows(ref[pl.ds(start, window)].astype(f32))
        h0[lo : lo + edge] = normed[:edge]
        u0[lo : lo + edge] = normed[tail:]

    def tap(l, lo):
        return w[l, :, :, lo : lo + wide].reshape(na * shard, wide)

    front, rear = (0, lead_rows), (lead_rows, edge)

    def now_part(l, now, span):
        lo, size = span
        pre[lo : lo + size] = bias_ref[l : l + 1, :] + jnp.dot(
            now[lo : lo + size], tap(l, wide), preferred_element_type=f32
        )

    def rest_part(l, earlier, span):
        lo, size = span
        total = pre[lo : lo + size] + jnp.dot(
            earlier[lo : lo + size], tap(l, 0), preferred_element_type=f32
        )
        hidden = (total[:, :dim] * jax.nn.sigmoid(total[:, dim:])).astype(bf16)
        mix = w[l, :, :, 2 * wide :].reshape(na * shard, dim)
        return lax.dot_general(hidden, mix, (((1,), (1,)), ((), ())), preferred_element_type=f32)

    enter(xin, pl.multiple_of(part - tail + half * edge, TILE), 0)
    home = norm_rows(xin[:part].astype(f32))
    u0[mine] = home
    if part > tail:
        h0[edge + tail : lead_rows] = home[: part - tail]
    relay(0, 0)
    relay(0, 1)
    pl.when(jnp.logical_not(near_cut))(x_pair.start)
    for k in range(2, len(orders[0][0])):
        relay(0, k)
    gather(0, 1)
    relay(1, 0)
    gather(0, 0)
    pl.when(has_last)(x_next.wait_recv)
    h0[edge : edge + tail] = norm_rows(xt[...].astype(f32))
    relay(1, 1)
    finish(0)

    def leave1(new, spot):
        state1[spot] = new
        u1[spot] = norm_rows(new)

    now_part(0, u0, front)
    relay(1, 2)
    grown = rest_part(0, h0, front)
    own_start = pl.multiple_of(part + half * edge, TILE)
    leave1(xin[pl.ds(own_start, edge)].astype(f32) + grown[:edge], pl.ds(place1(half), edge))
    leave1(xin[:part].astype(f32) + grown[edge:], mine)
    pl.when(has_next)(second_home.start)
    copy, there = second(half)
    pl.when(there)(copy.start)
    x_pair.wait_recv()
    enter(xp, 0, lead_rows)
    now_part(0, u0, rear)
    relay(1, 3)
    grown = rest_part(0, h0, rear)
    leave1(xp[tail:].astype(f32) + grown, pl.ds(place1(other), edge))
    copy, there = second(other)
    pl.when(there)(copy.start)
    for k in range(4, len(orders[1][0])):
        relay(1, k)
    gather(1, 1)
    gather(1, 0)
    finish(1)
    now_part(1, u1, front)
    now_part(1, u1, rear)
    relay(2, 0)

    def takes(s):
        @pl.when(jnp.logical_or(q + s > 0, down))
        def _():
            spot = pl.ds(place1(s), edge)
            halo(u1.at[spot], h1.at[spot], 3 + s, pair).wait_recv()

    def leave2(new, spot):
        normed = norm_rows(new)
        state2[spot] = new
        u2[spot] = normed
        return normed

    def leave2_edge(new, s):
        normed = leave2(new, pl.ds(place2(s), edge))

        @pl.when(s == 0)
        def _():
            h2[pl.ds(place2(1), edge)] = normed

        @pl.when(both(s == 1, up))
        def _():
            third.start()

    takes(lead)
    pl.when(has_last)(second_home.wait_recv)
    new = state1[:lead_rows] + rest_part(1, h1, front)
    leave2(new[edge:], mine)
    pl.when(has_far)(third_home.start)
    leave2_edge(new[:edge], lead)
    relay(2, 1)
    relay(2, 2)
    relay(2, 3)
    takes(1 - lead)
    leave2_edge(state1[lead_rows:] + rest_part(1, h1, rear), 1 - lead)
    for k in range(4, len(orders[2][0])):
        relay(2, k)
    gather(2, 1)
    gather(2, 0)
    finish(2)

    def takes_third(s):
        @pl.when(both(s == 0, down))
        def _():
            third.wait_recv()

    now_part(2, u2, rear)
    takes_third(other)
    oback[...] = (state2[lead_rows:] + rest_part(2, h2, rear)).astype(bf16)
    back.start()
    now_part(2, u2, front)
    takes_third(half)
    pl.when(had_far)(third_home.wait_recv)
    new = (state2[:lead_rows] + rest_part(2, h2, front)).astype(bf16)
    out_ref[edge_rows] = new[:edge]
    out_ref[:part] = new[edge:]
    for l in range(layers):
        for m in moves[l]:
            m.wait_send()
    for s in range(2):
        copy, there = second(s)
        pl.when(there)(copy.wait_send)
    pl.when(has_next)(second_home.wait_send)
    pl.when(has_next)(x_next.wait_send)
    pl.when(has_far)(third_home.wait_send)
    pl.when(up)(third.wait_send)
    x_pair.wait_send()
    back.wait_send()
    back.wait_recv()


def kernel_local(na, nb, sequence_input, w_prev, w_now, conv_bias, w_mix):
    rows, dim = sequence_input.shape
    layers, shard, wide = w_prev.shape
    tail = DILATIONS[0]
    part = 3 * tail // 2
    edge = (rows - part) // 2
    bf16, f32 = jnp.bfloat16, jnp.float32
    halos, copies = 8, shard // TILE + 6
    anywhere = pl.BlockSpec(memory_space=pl.ANY)
    vmem = pl.BlockSpec(memory_space=pltpu.VMEM)
    block = (rows, dim)
    return pl.pallas_call(
        functools.partial(block_kernel, na, nb, part, edge),
        out_shape=pltpu.VMEM((rows, dim), bf16),
        in_specs=[anywhere, anywhere, anywhere, vmem, anywhere],
        out_specs=vmem,
        scratch_shapes=[
            pltpu.VMEM((layers, na, shard, 2 * wide + dim), bf16),
            pltpu.VMEM(block, bf16),
            pltpu.VMEM((tail, dim), bf16),
            pltpu.VMEM((edge + tail, dim), bf16),
            pltpu.VMEM(block, f32),
            pltpu.VMEM(block, f32),
            pltpu.VMEM(block, bf16),
            pltpu.VMEM(block, bf16),
            pltpu.VMEM(block, bf16),
            pltpu.VMEM(block, bf16),
            pltpu.VMEM(block, bf16),
            pltpu.VMEM(block, bf16),
            pltpu.VMEM((rows, wide), f32),
            pltpu.VMEM((edge, dim), bf16),
            pltpu.SemaphoreType.DMA((layers, 3)),
            pltpu.SemaphoreType.DMA,
            pltpu.SemaphoreType.DMA((layers, copies)),
            pltpu.SemaphoreType.DMA((layers, copies)),
            pltpu.SemaphoreType.DMA((halos,)),
            pltpu.SemaphoreType.DMA((halos,)),
            pltpu.SemaphoreType.REGULAR,
        ],
        compiler_params=pltpu.CompilerParams(
            collective_id=0, has_side_effects=True, vmem_limit_bytes=56 * 2**20
        ),
    )(sequence_input, w_prev, w_now, conv_bias, jnp.swapaxes(w_mix, 1, 2))


def local(na, nb, sequence_input, w_prev, w_now, conv_bias, w_mix):
    rows = sequence_input.shape[0]
    shard = w_prev.shape[1]
    fits = (
        na == 4
        and nb % GROUP == 0
        and shard % TILE == 0
        and shard % (2 * TILE) == 0
        and shard >= 5 * TILE
        and rows % (4 * TILE) == 0
        and rows == 4 * DILATIONS[0]
        and DILATIONS[1] == rows
        and 2 * DILATIONS[2] == nb * rows
    )
    body = functools.partial(kernel_local, na, nb) if fits else plain_local
    return body(sequence_input, w_prev, w_now, conv_bias, w_mix)


def solution(mesh):
    return jax.shard_map(
        functools.partial(local, mesh.shape["seqa"], mesh.shape["seqb"]),
        mesh=mesh,
        in_specs=(
            P(("seqa", "seqb"), None),
            P(None, "seqa", None),
            P(None, "seqa", None),
            P(),
            P(None, None, "seqa"),
        ),
        out_specs=P(("seqa", "seqb"), None),
        check_vma=False,
    )
```

```python
import functools

import jax
import jax.numpy as jnp
from jax import lax
from jax.experimental import pallas as pl
from jax.experimental.pallas import tpu as pltpu
from jax.sharding import PartitionSpec as P

DILATIONS = (128, 512, 2048)
EPS = 1e-06
TILE = 16
GROUP = 4
MESH_ID = pl.DeviceIdType.MESH


def from_behind(value, axis, by):
    peers = lax.axis_size(axis)
    pairs = [(i, i + by) for i in range(peers) if 0 <= i + by < peers]
    return lax.ppermute(value, axis, pairs)


def norm_rows(values):
    scale = lax.rsqrt(jnp.mean(values * values, axis=1, keepdims=True) + EPS)
    return (values * scale).astype(jnp.bfloat16)


def block_prior(normed, dilation_step):
    rows = normed.shape[0]
    whole = dilation_step // rows
    part = dilation_step % rows
    pieces = []
    if part > 0:
        pieces.append(from_behind(normed[rows - part :], ("seqa", "seqb"), whole + 1))
    head = normed[: rows - part]
    if whole > 0:
        head = from_behind(head, ("seqa", "seqb"), whole)
    pieces.append(head)
    return jnp.concatenate(pieces, axis=0)


def one_layer(hidden_state, tap_prev, tap_now, bias, mixing, dilation_step):
    normed = norm_rows(hidden_state)
    earlier = block_prior(normed, dilation_step)
    dim = hidden_state.shape[1]
    pre = bias[None, :] + jnp.dot(
        earlier,
        lax.all_gather(tap_prev, "seqa", axis=0, tiled=True),
        preferred_element_type=jnp.float32,
    )
    pre = pre + jnp.dot(
        normed,
        lax.all_gather(tap_now, "seqa", axis=0, tiled=True),
        preferred_element_type=jnp.float32,
    )
    hidden = (pre[:, :dim] * jax.nn.sigmoid(pre[:, dim:])).astype(jnp.bfloat16)
    return hidden_state + jnp.dot(
        hidden,
        lax.all_gather(mixing, "seqa", axis=1, tiled=True),
        preferred_element_type=jnp.float32,
    )


def plain_local(sequence_input, w_prev, w_now, conv_bias, w_mix):
    state = sequence_input.astype(jnp.float32)
    for layer, step in enumerate(DILATIONS):
        state = one_layer(
            state, w_prev[layer], w_now[layer], conv_bias[layer], w_mix[layer], step
        )
    return state.astype(jnp.bfloat16)


def flip(value, bit):
    return value + bit - 2 * bit * ((value // bit) % 2)


def block_kernel(
    na, nb, part, edge,
    x_hbm, wp_hbm, wn_hbm, bias_ref, wm_hbm,
    out_ref,
    w, xin, xt, xp, state1, state2, u0, h0, u1, h1, u2, h2, pre, oback,
    load_sem, x_sem, send, recv, halo_send, halo_recv, hello,
):
    layers, dim = wp_hbm.shape[0], x_hbm.shape[1]
    wide = 2 * dim
    shard = wp_hbm.shape[1]
    rows = x_hbm.shape[0]
    n = na * nb
    tail = DILATIONS[0]
    window = edge + tail
    lead_rows = edge + part
    f32, bf16 = jnp.float32, jnp.bfloat16
    a, b = lax.axis_index("seqa"), lax.axis_index("seqb")
    me = a * nb + b
    a1, a2 = flip(a, 1), flip(a, 2)
    b1, b2 = flip(b, 1), flip(b, 2)
    tiles = shard // TILE
    zs = tiles // 5
    ys = tiles // 2 - zs
    yb, zb = b % 2, b // 2 % 2
    shares = [(ys, zs, None), (ys - 2, zs, None), (ys - 1, zs - 1, None)]

    def at(index):
        return (index // nb, index % nb)

    hop = DILATIONS[2] // rows
    half, q = b // hop, b % hop
    other = 1 - half
    pair = (a, (b + hop) % nb)
    wrap = (q + 1) // hop
    next_b = half * hop + (q + 1) % hop
    last_b = half * hop + (q + hop - 1) % hop
    after_a, before_a = (a + 1) % na, (a + na - 1) % na
    up, down = a + 1 < na, a > 0
    has_next, has_last = me + 1 < n, me > 0
    has_far, had_far = me + hop < n, me >= hop
    lead = jnp.where(q == 0, other, half)

    def place1(s):
        return pl.multiple_of(jnp.where(s == lead, 0, lead_rows), TILE)

    def place2(s):
        return pl.multiple_of(jnp.where(s == half, 0, lead_rows), TILE)

    loads = []
    for l in range(layers):
        loads.append([
            pltpu.make_async_copy(wp_hbm.at[l], w.at[l, a, :, pl.ds(0, wide)], load_sem.at[l, 0]),
            pltpu.make_async_copy(wn_hbm.at[l], w.at[l, a, :, pl.ds(wide, wide)], load_sem.at[l, 1]),
            pltpu.make_async_copy(wm_hbm.at[l], w.at[l, a, :, pl.ds(2 * wide, dim)], load_sem.at[l, 2]),
        ])
    for c in loads[0]:
        c.start()
    x_load = pltpu.make_async_copy(x_hbm, xin, x_sem)
    x_load.start()
    for l in range(1, layers):
        for c in loads[l]:
            c.start()

    z = b // 2
    inner = jnp.logical_and(z > 0, z < nb // 2 - 1)
    beside = (a, (b + nb - 2 + 4 * (z % 2)) % nb)

    def greet(sem, more):
        count = 4
        for dev in ((a1, b), (a2, b), (a, b1), (a, b2)):
            pl.semaphore_signal(sem, inc=1, device_id=dev, device_id_type=MESH_ID)
        for to, dev, come in [(inner, beside, inner)] + more:
            @pl.when(to)
            def _(dev=dev):
                pl.semaphore_signal(sem, inc=1, device_id=dev, device_id_type=MESH_ID)

            count = count + come.astype(jnp.int32)
        pl.semaphore_wait(sem, count)

    both = jnp.logical_and
    greet(pltpu.get_barrier_semaphore(), [
        (both(b == 0, down), (before_a, nb - 1), both(b == nb - 1, up)),
        (half == 0, pair, half == 1),
        (both(half == 0, down), (before_a, (b + hop) % nb), both(half == 1, up)),
        (q == 0, (a, last_b), wrap == 1),
        (both(q == 0, down), (before_a, last_b), both(wrap == 1, up)),
    ])

    def move(l, k, owner, start, size, dev):
        ref = w.at[l, owner, pl.ds(pl.multiple_of(start * TILE, TILE), size * TILE)]
        return pltpu.make_async_remote_copy(
            src_ref=ref, dst_ref=ref, send_sem=send.at[l, k], recv_sem=recv.at[l, k],
            device_id=dev, device_id_type=MESH_ID,
        )

    core, across, ynear, znear = (a1, b), (a2, b), (a, b1), (a, b2)
    moves, orders, lasts, sent = [], [], [], []
    fours, rest4 = tiles // 5, tiles - tiles // 5 * 4
    p = b % GROUP
    py, pz = flip(p, 1), flip(p, 2)
    pyz = flip(py, 2)
    plan = [(across, p, i) for i in range(fours)] + [(across, GROUP, i) for i in range(rest4)]
    plan += [(ynear, p, i) for i in range(fours)] + [(znear, p, i) for i in range(fours)]
    plan += [(ynear, pz, i) for i in range(fours)]
    x_own, x_rest, y_own, z_own, y_hop, plain = (
        0, fours, fours + rest4, 2 * fours + rest4, 3 * fours + rest4, 4 * fours + rest4
    )
    here = [
        move(0, k, a if dev is across else a2, block * fours + i, 1, dev)
        for k, (dev, block, i) in enumerate(plan)
    ]
    here.append(move(0, plain, a, 0, tiles, core))
    for k, (block, size) in enumerate(
        [(p, fours), (GROUP, rest4), (py, fours), (pz, fours), (pyz, fours)]
    ):
        here.append(move(0, plain + 1 + k, a2, block * fours, size, core))
    moves.append(here)
    sent += [(m, None) for m in here]
    orders.append(([(2, 0)] * (fours + rest4), None, None, None, None, None))
    lasts.append(plain)

    def arrive(k, then=()):
        moves[0][k].wait_recv()
        for t in then:
            moves[0][t].start()

    def layer0_own():
        for i in range(fours):
            arrive(x_own + i, (y_own + i, z_own + i))
        moves[0][plain + 1].start()

    def layer0_rest():
        for i in range(max(fours, rest4)):
            if i < rest4:
                arrive(x_rest + i)
            if i < fours:
                arrive(z_own + i, (y_hop + i,))
        moves[0][plain + 2].start()
        moves[0][plain + 4].start()
        for i in range(fours):
            arrive(y_own + i)
        moves[0][plain + 3].start()

    def layer0_hops():
        for i in range(fours):
            arrive(y_hop + i)
        moves[0][plain + 5].start()

    for l, (y, z, spread) in enumerate(shares[1:], 1):
        pick = 0 if spread is None else 1
        rest = tiles - 2 * (y + z + pick)
        swap = 2 * (y + z)
        own = (yb * y, 2 * y + zb * z, swap + 2 * pick, swap + zb, swap + 1 - zb)
        theirs = ((1 - yb) * y, 2 * y + (1 - zb) * z)
        sizes = (y, z, rest, pick, pick)
        order = [(1, i) for i in range(z)] + [(3, i) for i in range(pick)]
        order += [(0, i) for i in range(y)] + [(2, i) for i in range(rest)] + [(4, i) for i in range(pick)]
        mine = spread and spread(a // 2, yb)
        away = spread and jnp.logical_not(spread(1 - a // 2, yb))
        here = [(move(l, k, a, own[f] + i, 1, across), away if f == 4 else None) for k, (f, i) in enumerate(order)]
        relays = {}
        for k, (f, i) in enumerate(order):
            if f in (0, 1, 3):
                relays[k] = len(here)
                here.append((
                    move(l, len(here), a2, own[f] + i, 1, znear if f else ynear), mine if f == 3 else None
                ))
        last = len(here)
        here.append((move(l, last, a, 0, tiles, core), None))
        local = {}
        for f in range(5):
            if sizes[f]:
                local[f] = len(here)
                here.append((move(l, len(here), a2, own[f], sizes[f], core), None))
        for f in range(2):
            here.append((move(l, len(here), a2, theirs[f], sizes[f], core), None))
        moves.append([m for m, _ in here])
        sent += here
        orders.append((order, sizes, relays, local, mine, away))
        lasts.append(last)

    def maybe(there, do):
        if there is None:
            do()
        else:
            pl.when(there)(do)

    def start_weights(l):
        order, away = orders[l][0], orders[l][5]
        for k, (f, _) in enumerate(order):
            maybe(away if f == 4 else None, moves[l][k].start)
        moves[l][lasts[l]].start()

    def relay(l, k):
        order, sizes, relays, local, mine, _ = orders[l]
        f, i = order[k]

        def here():
            moves[l][k].wait_recv()
            if k in relays:
                maybe(mine if f == 3 else None, moves[l][relays[k]].start)
            if i == sizes[f] - 1:
                moves[l][local[f]].start()

        maybe(jnp.logical_not(mine) if f == 4 else None, here)

    def gather(l, f):
        order, sizes, relays, local, mine, _ = orders[l]
        for k in relays:
            if order[k][0] == f:
                moves[l][relays[k]].wait_recv()
        moves[l][len(moves[l]) - 2 + f].start()
        for k in relays:
            if f == 1 and order[k][0] == 3:
                @pl.when(mine)
                def _(k=k):
                    moves[l][relays[k]].wait_recv()
                    moves[l][local[4]].start()

    def finish(l):
        for k in range(lasts[l], len(moves[l])):
            moves[l][k].wait_recv()

    def halo(src, dst, slot, dev):
        return pltpu.make_async_remote_copy(
            src_ref=src, dst_ref=dst, send_sem=halo_send.at[slot], recv_sem=halo_recv.at[slot],
            device_id=dev, device_id_type=MESH_ID,
        )

    mine = pl.ds(edge, part)
    x_next = halo(xin.at[pl.ds(rows - tail, tail)], xt, 0, at((me + 1) % n))
    cut = window // TILE // 2 * TILE
    x_pair = [
        halo(
            xin.at[pl.ds(pl.multiple_of(part - tail + other * edge + lo, TILE), size)],
            xp.at[pl.ds(lo, size)], slot, pair,
        )
        for lo, size, slot in ((0, cut, 1), (cut, window - cut, 8))
    ]
    second_home = halo(u1.at[mine], h1.at[mine], 2, at((me + 1) % n))

    def second(s):
        to = s + wrap
        slot = to % 2
        return halo(
            u1.at[pl.ds(place1(s), edge)], h1.at[pl.ds(place1_at_next(slot), edge)],
            3 + slot, ((a + to // 2) % na, next_b),
        ), a + to // 2 < na

    def place1_at_next(slot):
        first = jnp.where(wrap == 1, other, half)
        return pl.multiple_of(jnp.where(slot == first, 0, lead_rows), TILE)

    third_home = halo(u2.at[mine], h2.at[mine], 5, at((me + hop) % n))
    third = halo(u2.at[pl.ds(place2(1), edge)], h2.at[pl.ds(place2(0), edge)], 6, (after_a, b))
    edge_rows = pl.ds(pl.multiple_of(part + half * edge, TILE), edge)
    back = halo(oback, out_ref.at[edge_rows], 7, pair)
    near_cut = (b // 2) % 2 != half

    for c in loads[0]:
        c.wait()
    start_weights(0)
    x_load.wait()
    greet(hello, [])
    pl.when(has_next)(x_next.start)

    def pair_rest():
        pl.when(jnp.logical_not(near_cut))(x_pair[0].start)
        pl.when(jnp.logical_not(near_cut))(x_pair[1].start)

    pl.when(near_cut)(x_pair[0].start)
    pl.when(near_cut)(x_pair[1].start)
    for l in range(1, layers):
        for c in loads[l]:
            c.wait()
        start_weights(l)

    @pl.when(me == 0)
    def _():
        xt[...] = jnp.zeros(xt.shape, xt.dtype)
        h1[mine] = jnp.zeros((part, dim), h1.dtype)

    @pl.when(both(a == 0, q == 0))
    def _():
        h1[pl.ds(place1(0), edge)] = jnp.zeros((edge, dim), h1.dtype)

    @pl.when(a == 0)
    def _():
        h2[pl.ds(place2(0), edge)] = jnp.zeros((edge, dim), h2.dtype)

    @pl.when(jnp.logical_not(had_far))
    def _():
        h2[mine] = jnp.zeros((part, dim), h2.dtype)

    def enter(ref, start, lo):
        normed = norm_rows(ref[pl.ds(start, window)].astype(f32))
        h0[lo : lo + edge] = normed[:edge]
        u0[lo : lo + edge] = normed[tail:]

    def tap(l, lo):
        return w[l, :, :, lo : lo + wide].reshape(na * shard, wide)

    front, rear = (0, lead_rows), (lead_rows, edge)

    def now_part(l, now, span):
        lo, size = span
        pre[lo : lo + size] = bias_ref[l : l + 1, :] + jnp.dot(
            now[lo : lo + size], tap(l, wide), preferred_element_type=f32
        )

    def rest_part(l, earlier, span):
        lo, size = span
        total = pre[lo : lo + size] + jnp.dot(
            earlier[lo : lo + size], tap(l, 0), preferred_element_type=f32
        )
        hidden = (total[:, :dim] * jax.nn.sigmoid(total[:, dim:])).astype(bf16)
        mix = w[l, :, :, 2 * wide :].reshape(na * shard, dim)
        return lax.dot_general(hidden, mix, (((1,), (1,)), ((), ())), preferred_element_type=f32)

    enter(xin, pl.multiple_of(part - tail + half * edge, TILE), 0)
    home = norm_rows(xin[:part].astype(f32))
    u0[mine] = home
    if part > tail:
        h0[edge + tail : lead_rows] = home[: part - tail]
    layer0_own()
    pair_rest()
    layer0_rest()
    relay(1, 0)
    layer0_hops()
    pl.when(has_last)(x_next.wait_recv)
    h0[edge : edge + tail] = norm_rows(xt[...].astype(f32))
    relay(1, 1)
    finish(0)

    def leave1(new, spot):
        state1[spot] = new
        u1[spot] = norm_rows(new)

    now_part(0, u0, front)
    relay(1, 2)
    grown = rest_part(0, h0, front)
    own_start = pl.multiple_of(part + half * edge, TILE)
    leave1(xin[pl.ds(own_start, edge)].astype(f32) + grown[:edge], pl.ds(place1(half), edge))
    leave1(xin[:part].astype(f32) + grown[edge:], mine)
    pl.when(has_next)(second_home.start)
    copy, there = second(half)
    pl.when(there)(copy.start)
    for c in x_pair:
        c.wait_recv()
    enter(xp, 0, lead_rows)
    now_part(0, u0, rear)
    relay(1, 3)
    grown = rest_part(0, h0, rear)
    leave1(xp[tail:].astype(f32) + grown, pl.ds(place1(other), edge))
    copy, there = second(other)
    pl.when(there)(copy.start)
    for k in range(4, len(orders[1][0])):
        relay(1, k)
    gather(1, 1)
    gather(1, 0)
    finish(1)
    now_part(1, u1, front)
    now_part(1, u1, rear)
    relay(2, 0)

    def takes(s):
        @pl.when(jnp.logical_or(q + s > 0, down))
        def _():
            spot = pl.ds(place1(s), edge)
            halo(u1.at[spot], h1.at[spot], 3 + s, pair).wait_recv()

    def leave2(new, spot):
        normed = norm_rows(new)
        state2[spot] = new
        u2[spot] = normed
        return normed

    def leave2_edge(new, s):
        normed = leave2(new, pl.ds(place2(s), edge))

        @pl.when(s == 0)
        def _():
            h2[pl.ds(place2(1), edge)] = normed

        @pl.when(both(s == 1, up))
        def _():
            third.start()

    relay(2, 1)
    def middle():
        relay(2, 2)

    pl.when(b % 2 == 0)(middle)
    takes(lead)
    pl.when(has_last)(second_home.wait_recv)
    new = state1[:lead_rows] + rest_part(1, h1, front)
    leave2(new[edge:], mine)
    pl.when(has_far)(third_home.start)
    leave2_edge(new[:edge], lead)
    pl.when(jnp.logical_not(b % 2 == 0))(middle)
    relay(2, 3)

    def last_relays():
        for k in range(4, len(orders[2][0])):
            relay(2, k)
        gather(2, 1)
        gather(2, 0)

    pl.when(q == 0)(last_relays)

    takes(1 - lead)
    leave2_edge(state1[lead_rows:] + rest_part(1, h1, rear), 1 - lead)
    pl.when(q > 0)(last_relays)
    finish(2)

    def takes_third(s):
        @pl.when(both(s == 0, down))
        def _():
            third.wait_recv()

    def end_rear():
        now_part(2, u2, rear)
        takes_third(other)
        oback[...] = (state2[lead_rows:] + rest_part(2, h2, rear)).astype(bf16)
        back.start()

    def end_front():
        now_part(2, u2, front)
        takes_third(half)
        pl.when(had_far)(third_home.wait_recv)
        new = (state2[:lead_rows] + rest_part(2, h2, front)).astype(bf16)
        out_ref[edge_rows] = new[:edge]
        out_ref[:part] = new[edge:]

    early = jnp.logical_or(near_cut, both(half == 0, a >= na // 2) | both(half == 1, a >= na // 2))
    pl.when(early)(end_rear)
    end_front()
    pl.when(jnp.logical_not(early))(end_rear)
    for m, there in sent:
        maybe(there, m.wait_send)
    for s in range(2):
        copy, there = second(s)
        pl.when(there)(copy.wait_send)
    pl.when(has_next)(second_home.wait_send)
    pl.when(has_next)(x_next.wait_send)
    pl.when(has_far)(third_home.wait_send)
    pl.when(up)(third.wait_send)
    for c in x_pair:
        c.wait_send()
    back.wait_send()
    back.wait_recv()


def kernel_local(na, nb, sequence_input, w_prev, w_now, conv_bias, w_mix):
    rows, dim = sequence_input.shape
    layers, shard, wide = w_prev.shape
    tail = DILATIONS[0]
    part = 3 * tail // 2
    edge = (rows - part) // 2
    bf16, f32 = jnp.bfloat16, jnp.float32
    halos, copies = 9, 2 * (shard // TILE)
    anywhere = pl.BlockSpec(memory_space=pl.ANY)
    vmem = pl.BlockSpec(memory_space=pltpu.VMEM)
    block = (rows, dim)
    return pl.pallas_call(
        functools.partial(block_kernel, na, nb, part, edge),
        out_shape=pltpu.VMEM((rows, dim), bf16),
        in_specs=[anywhere, anywhere, anywhere, vmem, anywhere],
        out_specs=vmem,
        scratch_shapes=[
            pltpu.VMEM((layers, na, shard, 2 * wide + dim), bf16),
            pltpu.VMEM(block, bf16),
            pltpu.VMEM((tail, dim), bf16),
            pltpu.VMEM((edge + tail, dim), bf16),
            pltpu.VMEM(block, f32),
            pltpu.VMEM(block, f32),
            pltpu.VMEM(block, bf16),
            pltpu.VMEM(block, bf16),
            pltpu.VMEM(block, bf16),
            pltpu.VMEM(block, bf16),
            pltpu.VMEM(block, bf16),
            pltpu.VMEM(block, bf16),
            pltpu.VMEM((rows, wide), f32),
            pltpu.VMEM((edge, dim), bf16),
            pltpu.SemaphoreType.DMA((layers, 3)),
            pltpu.SemaphoreType.DMA,
            pltpu.SemaphoreType.DMA((layers, copies)),
            pltpu.SemaphoreType.DMA((layers, copies)),
            pltpu.SemaphoreType.DMA((halos,)),
            pltpu.SemaphoreType.DMA((halos,)),
            pltpu.SemaphoreType.REGULAR,
        ],
        compiler_params=pltpu.CompilerParams(
            collective_id=0, has_side_effects=True, vmem_limit_bytes=56 * 2**20
        ),
    )(sequence_input, w_prev, w_now, conv_bias, jnp.swapaxes(w_mix, 1, 2))


def local(na, nb, sequence_input, w_prev, w_now, conv_bias, w_mix):
    rows = sequence_input.shape[0]
    shard = w_prev.shape[1]
    fits = (
        na == 4
        and nb % GROUP == 0
        and shard % TILE == 0
        and shard % (2 * TILE) == 0
        and shard >= 5 * TILE
        and rows % (4 * TILE) == 0
        and rows == 4 * DILATIONS[0]
        and DILATIONS[1] == rows
        and 2 * DILATIONS[2] == nb * rows
    )
    body = functools.partial(kernel_local, na, nb) if fits else plain_local
    return body(sequence_input, w_prev, w_now, conv_bias, w_mix)


def solution(mesh):
    return jax.shard_map(
        functools.partial(local, mesh.shape["seqa"], mesh.shape["seqb"]),
        mesh=mesh,
        in_specs=(
            P(("seqa", "seqb"), None),
            P(None, "seqa", None),
            P(None, "seqa", None),
            P(),
            P(None, None, "seqa"),
        ),
        out_specs=P(("seqa", "seqb"), None),
        check_vma=False,
    )
```

```python
import functools

import jax
import jax.numpy as jnp
from jax import lax
from jax.experimental import pallas as pl
from jax.experimental.pallas import tpu as pltpu
from jax.sharding import PartitionSpec as P

DILATIONS = (128, 512, 2048)
EPS = 1e-06
TILE = 16
GROUP = 4
MESH_ID = pl.DeviceIdType.MESH


def from_behind(value, axis, by):
    peers = lax.axis_size(axis)
    pairs = [(i, i + by) for i in range(peers) if 0 <= i + by < peers]
    return lax.ppermute(value, axis, pairs)


def norm_rows(values):
    scale = lax.rsqrt(jnp.mean(values * values, axis=1, keepdims=True) + EPS)
    return (values * scale).astype(jnp.bfloat16)


def block_prior(normed, dilation_step):
    rows = normed.shape[0]
    whole = dilation_step // rows
    part = dilation_step % rows
    pieces = []
    if part > 0:
        pieces.append(from_behind(normed[rows - part :], ("seqa", "seqb"), whole + 1))
    head = normed[: rows - part]
    if whole > 0:
        head = from_behind(head, ("seqa", "seqb"), whole)
    pieces.append(head)
    return jnp.concatenate(pieces, axis=0)


def one_layer(hidden_state, tap_prev, tap_now, bias, mixing, dilation_step):
    normed = norm_rows(hidden_state)
    earlier = block_prior(normed, dilation_step)
    dim = hidden_state.shape[1]
    pre = bias[None, :] + jnp.dot(
        earlier,
        lax.all_gather(tap_prev, "seqa", axis=0, tiled=True),
        preferred_element_type=jnp.float32,
    )
    pre = pre + jnp.dot(
        normed,
        lax.all_gather(tap_now, "seqa", axis=0, tiled=True),
        preferred_element_type=jnp.float32,
    )
    hidden = (pre[:, :dim] * jax.nn.sigmoid(pre[:, dim:])).astype(jnp.bfloat16)
    return hidden_state + jnp.dot(
        hidden,
        lax.all_gather(mixing, "seqa", axis=1, tiled=True),
        preferred_element_type=jnp.float32,
    )


def plain_local(sequence_input, w_prev, w_now, conv_bias, w_mix):
    state = sequence_input.astype(jnp.float32)
    for layer, step in enumerate(DILATIONS):
        state = one_layer(
            state, w_prev[layer], w_now[layer], conv_bias[layer], w_mix[layer], step
        )
    return state.astype(jnp.bfloat16)


def flip(value, bit):
    return value + bit - 2 * bit * ((value // bit) % 2)


def block_kernel(
    na, nb, part, edge,
    x_hbm, wp_hbm, wn_hbm, bias_ref, wm_hbm,
    out_ref,
    w, xin, xt, xp, state1, state2, u0, h0, u1, h1, u2, h2, pre, oback,
    load_sem, x_sem, send, recv, halo_send, halo_recv, hello,
):
    layers, dim = wp_hbm.shape[0], x_hbm.shape[1]
    wide = 2 * dim
    shard = wp_hbm.shape[1]
    rows = x_hbm.shape[0]
    n = na * nb
    tail = DILATIONS[0]
    window = edge + tail
    lead_rows = edge + part
    f32, bf16 = jnp.float32, jnp.bfloat16
    a, b = lax.axis_index("seqa"), lax.axis_index("seqb")
    me = a * nb + b
    a1, a2 = flip(a, 1), flip(a, 2)
    b1, b2 = flip(b, 1), flip(b, 2)
    tiles = shard // TILE
    zs = tiles // 5
    ys = tiles // 2 - zs
    yb, zb = b % 2, b // 2 % 2
    shares = [(ys, zs, None), (ys - 2, zs, None), (ys - 1, zs - 1, None)]

    def at(index):
        return (index // nb, index % nb)

    hop = DILATIONS[2] // rows
    half, q = b // hop, b % hop
    other = 1 - half
    pair = (a, (b + hop) % nb)
    wrap = (q + 1) // hop
    next_b = half * hop + (q + 1) % hop
    last_b = half * hop + (q + hop - 1) % hop
    after_a, before_a = (a + 1) % na, (a + na - 1) % na
    up, down = a + 1 < na, a > 0
    has_next, has_last = me + 1 < n, me > 0
    has_far, had_far = me + hop < n, me >= hop
    lead = jnp.where(q == 0, other, half)

    def place1(s):
        return pl.multiple_of(jnp.where(s == lead, 0, lead_rows), TILE)

    def place2(s):
        return pl.multiple_of(jnp.where(s == half, 0, lead_rows), TILE)

    loads = []
    for l in range(layers):
        loads.append([
            pltpu.make_async_copy(wp_hbm.at[l], w.at[l, a, :, pl.ds(0, wide)], load_sem.at[l, 0]),
            pltpu.make_async_copy(wn_hbm.at[l], w.at[l, a, :, pl.ds(wide, wide)], load_sem.at[l, 1]),
            pltpu.make_async_copy(wm_hbm.at[l], w.at[l, a, :, pl.ds(2 * wide, dim)], load_sem.at[l, 2]),
        ])
    for c in loads[0]:
        c.start()
    x_load = pltpu.make_async_copy(x_hbm, xin, x_sem)
    x_load.start()
    for l in range(1, layers):
        for c in loads[l]:
            c.start()

    z = b // 2
    inner = jnp.logical_and(z > 0, z < nb // 2 - 1)
    beside = (a, (b + nb - 2 + 4 * (z % 2)) % nb)

    def greet(sem, more):
        count = 4
        for dev in ((a1, b), (a2, b), (a, b1), (a, b2)):
            pl.semaphore_signal(sem, inc=1, device_id=dev, device_id_type=MESH_ID)
        for to, dev, come in [(inner, beside, inner)] + more:
            @pl.when(to)
            def _(dev=dev):
                pl.semaphore_signal(sem, inc=1, device_id=dev, device_id_type=MESH_ID)

            count = count + come.astype(jnp.int32)
        pl.semaphore_wait(sem, count)

    both = jnp.logical_and
    greet(pltpu.get_barrier_semaphore(), [
        (both(b == 0, down), (before_a, nb - 1), both(b == nb - 1, up)),
        (half == 0, pair, half == 1),
        (both(half == 0, down), (before_a, (b + hop) % nb), both(half == 1, up)),
        (q == 0, (a, last_b), wrap == 1),
        (both(q == 0, down), (before_a, last_b), both(wrap == 1, up)),
    ])

    def move(l, k, owner, start, size, dev):
        ref = w.at[l, owner, pl.ds(pl.multiple_of(start * TILE, TILE), size * TILE)]
        return pltpu.make_async_remote_copy(
            src_ref=ref, dst_ref=ref, send_sem=send.at[l, k], recv_sem=recv.at[l, k],
            device_id=dev, device_id_type=MESH_ID,
        )

    core, across, ynear, znear = (a1, b), (a2, b), (a, b1), (a, b2)
    moves, orders, lasts, sent = [], [], [], []
    fours, rest4 = tiles // 5, tiles - tiles // 5 * 4
    p = b % GROUP
    py, pz = flip(p, 1), flip(p, 2)
    pyz = flip(py, 2)
    plan = [(across, p, i) for i in range(fours)] + [(across, GROUP, i) for i in range(rest4)]
    plan += [(ynear, p, i) for i in range(fours)] + [(znear, p, i) for i in range(fours)]
    plan += [(ynear, pz, i) for i in range(fours)]
    x_own, x_rest, y_own, z_own, y_hop, plain = (
        0, fours, fours + rest4, 2 * fours + rest4, 3 * fours + rest4, 4 * fours + rest4
    )
    here = [
        move(0, k, a if dev is across else a2, block * fours + i, 1, dev)
        for k, (dev, block, i) in enumerate(plan)
    ]
    here.append(move(0, plain, a, 0, tiles, core))
    for k, (block, size) in enumerate(
        [(p, fours), (GROUP, rest4), (py, fours), (pz, fours), (pyz, fours)]
    ):
        here.append(move(0, plain + 1 + k, a2, block * fours, size, core))
    moves.append(here)
    sent += [(m, None) for m in here]
    orders.append(([(2, 0)] * (fours + rest4), None, None, None, None, None))
    lasts.append(plain)

    def arrive(k, then=()):
        moves[0][k].wait_recv()
        for t in then:
            moves[0][t].start()

    def layer0_own():
        for i in range(fours):
            arrive(x_own + i, (y_own + i, z_own + i))
        moves[0][plain + 1].start()

    def layer0_rest():
        for i in range(max(fours, rest4)):
            if i < rest4:
                arrive(x_rest + i)
            if i < fours:
                arrive(z_own + i, (y_hop + i,))
        moves[0][plain + 2].start()
        moves[0][plain + 4].start()
        for i in range(fours):
            arrive(y_own + i)
        moves[0][plain + 3].start()

    def layer0_hops():
        for i in range(fours):
            arrive(y_hop + i)
        moves[0][plain + 5].start()

    for l, (y, z, spread) in enumerate(shares[1:], 1):
        pick = 0 if spread is None else 1
        rest = tiles - 2 * (y + z + pick)
        swap = 2 * (y + z)
        own = (yb * y, 2 * y + zb * z, swap + 2 * pick, swap + zb, swap + 1 - zb)
        theirs = ((1 - yb) * y, 2 * y + (1 - zb) * z)
        sizes = (y, z, rest, pick, pick)
        order = [(1, i) for i in range(z)] + [(3, i) for i in range(pick)]
        order += [(0, i) for i in range(y)] + [(2, i) for i in range(rest)] + [(4, i) for i in range(pick)]
        mine = spread and spread(a // 2, yb)
        away = spread and jnp.logical_not(spread(1 - a // 2, yb))
        here = [(move(l, k, a, own[f] + i, 1, across), away if f == 4 else None) for k, (f, i) in enumerate(order)]
        relays = {}
        for k, (f, i) in enumerate(order):
            if f in (0, 1, 3):
                relays[k] = len(here)
                here.append((
                    move(l, len(here), a2, own[f] + i, 1, znear if f else ynear), mine if f == 3 else None
                ))
        last = len(here)
        here.append((move(l, last, a, 0, tiles, core), None))
        local = {}
        for f in range(5):
            if sizes[f]:
                local[f] = len(here)
                here.append((move(l, len(here), a2, own[f], sizes[f], core), None))
        for f in range(2):
            here.append((move(l, len(here), a2, theirs[f], sizes[f], core), None))
        moves.append([m for m, _ in here])
        sent += here
        orders.append((order, sizes, relays, local, mine, away))
        lasts.append(last)

    def maybe(there, do):
        if there is None:
            do()
        else:
            pl.when(there)(do)

    def start_weights(l):
        order, away = orders[l][0], orders[l][5]
        for k, (f, _) in enumerate(order):
            maybe(away if f == 4 else None, moves[l][k].start)
        moves[l][lasts[l]].start()

    def relay(l, k):
        order, sizes, relays, local, mine, _ = orders[l]
        f, i = order[k]

        def here():
            moves[l][k].wait_recv()
            if k in relays:
                maybe(mine if f == 3 else None, moves[l][relays[k]].start)
            if i == sizes[f] - 1:
                moves[l][local[f]].start()

        maybe(jnp.logical_not(mine) if f == 4 else None, here)

    def gather(l, f):
        order, sizes, relays, local, mine, _ = orders[l]
        for k in relays:
            if order[k][0] == f:
                moves[l][relays[k]].wait_recv()
        moves[l][len(moves[l]) - 2 + f].start()
        for k in relays:
            if f == 1 and order[k][0] == 3:
                @pl.when(mine)
                def _(k=k):
                    moves[l][relays[k]].wait_recv()
                    moves[l][local[4]].start()

    def finish(l):
        for k in range(lasts[l], len(moves[l])):
            moves[l][k].wait_recv()

    def halo(src, dst, slot, dev):
        return pltpu.make_async_remote_copy(
            src_ref=src, dst_ref=dst, send_sem=halo_send.at[slot], recv_sem=halo_recv.at[slot],
            device_id=dev, device_id_type=MESH_ID,
        )

    mine = pl.ds(edge, part)
    x_next = halo(xin.at[pl.ds(rows - tail, tail)], xt, 0, at((me + 1) % n))
    cut = window // TILE // 2 * TILE
    x_pair = [
        halo(
            xin.at[pl.ds(pl.multiple_of(part - tail + other * edge + lo, TILE), size)],
            xp.at[pl.ds(lo, size)], slot, pair,
        )
        for lo, size, slot in ((0, cut, 1), (cut, window - cut, 8))
    ]
    second_home = halo(u1.at[mine], h1.at[mine], 2, at((me + 1) % n))

    def second(s):
        to = s + wrap
        slot = to % 2
        return halo(
            u1.at[pl.ds(place1(s), edge)], h1.at[pl.ds(place1_at_next(slot), edge)],
            3 + slot, ((a + to // 2) % na, next_b),
        ), a + to // 2 < na

    def place1_at_next(slot):
        first = jnp.where(wrap == 1, other, half)
        return pl.multiple_of(jnp.where(slot == first, 0, lead_rows), TILE)

    third_home = halo(u2.at[mine], h2.at[mine], 5, at((me + hop) % n))
    third = halo(u2.at[pl.ds(place2(1), edge)], h2.at[pl.ds(place2(0), edge)], 6, (after_a, b))
    edge_rows = pl.ds(pl.multiple_of(part + half * edge, TILE), edge)
    back = halo(oback, out_ref.at[edge_rows], 7, pair)
    near_cut = (b // 2) % 2 != half

    for c in loads[0]:
        c.wait()
    start_weights(0)
    x_load.wait()
    greet(hello, [])
    pl.when(has_next)(x_next.start)

    def pair_rest():
        pl.when(jnp.logical_not(near_cut))(x_pair[0].start)
        pl.when(jnp.logical_not(near_cut))(x_pair[1].start)

    pl.when(near_cut)(x_pair[0].start)
    pl.when(near_cut)(x_pair[1].start)
    for l in range(1, layers):
        for c in loads[l]:
            c.wait()
        start_weights(l)

    @pl.when(me == 0)
    def _():
        xt[...] = jnp.zeros(xt.shape, xt.dtype)
        h1[mine] = jnp.zeros((part, dim), h1.dtype)

    @pl.when(both(a == 0, q == 0))
    def _():
        h1[pl.ds(place1(0), edge)] = jnp.zeros((edge, dim), h1.dtype)

    @pl.when(a == 0)
    def _():
        h2[pl.ds(place2(0), edge)] = jnp.zeros((edge, dim), h2.dtype)

    @pl.when(jnp.logical_not(had_far))
    def _():
        h2[mine] = jnp.zeros((part, dim), h2.dtype)

    def enter(ref, start, lo):
        normed = norm_rows(ref[pl.ds(start, window)].astype(f32))
        h0[lo : lo + edge] = normed[:edge]
        u0[lo : lo + edge] = normed[tail:]

    def tap(l, lo):
        return w[l, :, :, lo : lo + wide].reshape(na * shard, wide)

    front, rear = (0, lead_rows), (lead_rows, edge)
    lead_span, home_span = (0, edge), (edge, part)

    def now_part(l, now, span):
        lo, size = span
        pre[lo : lo + size] = bias_ref[l : l + 1, :] + jnp.dot(
            now[lo : lo + size], tap(l, wide), preferred_element_type=f32
        )

    def rest_part(l, earlier, span):
        lo, size = span
        total = pre[lo : lo + size] + jnp.dot(
            earlier[lo : lo + size], tap(l, 0), preferred_element_type=f32
        )
        hidden = (total[:, :dim] * jax.nn.sigmoid(total[:, dim:])).astype(bf16)
        mix = w[l, :, :, 2 * wide :].reshape(na * shard, dim)
        return lax.dot_general(hidden, mix, (((1,), (1,)), ((), ())), preferred_element_type=f32)

    enter(xin, pl.multiple_of(part - tail + half * edge, TILE), 0)
    home = norm_rows(xin[:part].astype(f32))
    u0[mine] = home
    if part > tail:
        h0[edge + tail : lead_rows] = home[: part - tail]
    layer0_own()
    pair_rest()
    layer0_rest()
    relay(1, 0)
    layer0_hops()
    pl.when(has_last)(x_next.wait_recv)
    h0[edge : edge + tail] = norm_rows(xt[...].astype(f32))
    relay(1, 1)
    finish(0)

    def leave1(new, spot):
        state1[spot] = new
        u1[spot] = norm_rows(new)

    now_part(0, u0, front)
    relay(1, 2)
    grown = rest_part(0, h0, front)
    own_start = pl.multiple_of(part + half * edge, TILE)
    leave1(xin[pl.ds(own_start, edge)].astype(f32) + grown[:edge], pl.ds(place1(half), edge))
    leave1(xin[:part].astype(f32) + grown[edge:], mine)
    pl.when(has_next)(second_home.start)
    copy, there = second(half)
    pl.when(there)(copy.start)
    for c in x_pair:
        c.wait_recv()
    enter(xp, 0, lead_rows)
    now_part(0, u0, rear)
    relay(1, 3)
    grown = rest_part(0, h0, rear)
    leave1(xp[tail:].astype(f32) + grown, pl.ds(place1(other), edge))
    copy, there = second(other)
    pl.when(there)(copy.start)
    for k in range(4, len(orders[1][0])):
        relay(1, k)
    gather(1, 1)
    gather(1, 0)
    finish(1)
    now_part(1, u1, front)
    now_part(1, u1, rear)
    relay(2, 0)

    def takes(s):
        @pl.when(jnp.logical_or(q + s > 0, down))
        def _():
            spot = pl.ds(place1(s), edge)
            halo(u1.at[spot], h1.at[spot], 3 + s, pair).wait_recv()

    def leave2(new, spot):
        normed = norm_rows(new)
        state2[spot] = new
        u2[spot] = normed
        return normed

    def leave2_edge(new, s):
        normed = leave2(new, pl.ds(place2(s), edge))

        @pl.when(s == 0)
        def _():
            h2[pl.ds(place2(1), edge)] = normed

        @pl.when(both(s == 1, up))
        def _():
            third.start()

    relay(2, 1)
    def middle():
        relay(2, 2)

    pl.when(b % 2 == 0)(middle)
    pl.when(has_last)(second_home.wait_recv)
    leave2(state1[mine] + rest_part(1, h1, home_span), mine)
    pl.when(has_far)(third_home.start)
    takes(lead)
    leave2_edge(state1[:edge] + rest_part(1, h1, lead_span), lead)
    pl.when(jnp.logical_not(b % 2 == 0))(middle)
    relay(2, 3)

    def last_relays():
        for k in range(4, len(orders[2][0])):
            relay(2, k)
        gather(2, 1)
        gather(2, 0)

    pl.when(q == 0)(last_relays)

    takes(1 - lead)
    leave2_edge(state1[lead_rows:] + rest_part(1, h1, rear), 1 - lead)
    pl.when(q > 0)(last_relays)
    finish(2)

    def takes_third(s):
        @pl.when(both(s == 0, down))
        def _():
            third.wait_recv()

    def end_rear():
        now_part(2, u2, rear)
        takes_third(other)
        oback[...] = (state2[lead_rows:] + rest_part(2, h2, rear)).astype(bf16)
        back.start()

    def end_front():
        now_part(2, u2, front)
        takes_third(half)
        out_ref[edge_rows] = (state2[:edge] + rest_part(2, h2, lead_span)).astype(bf16)
        pl.when(had_far)(third_home.wait_recv)
        out_ref[:part] = (state2[mine] + rest_part(2, h2, home_span)).astype(bf16)

    early = jnp.logical_or(near_cut, both(half == 0, a >= na // 2) | both(half == 1, a >= na // 2))
    pl.when(early)(end_rear)
    end_front()
    pl.when(jnp.logical_not(early))(end_rear)
    for m, there in sent:
        maybe(there, m.wait_send)
    for s in range(2):
        copy, there = second(s)
        pl.when(there)(copy.wait_send)
    pl.when(has_next)(second_home.wait_send)
    pl.when(has_next)(x_next.wait_send)
    pl.when(has_far)(third_home.wait_send)
    pl.when(up)(third.wait_send)
    for c in x_pair:
        c.wait_send()
    back.wait_send()
    back.wait_recv()


def kernel_local(na, nb, sequence_input, w_prev, w_now, conv_bias, w_mix):
    rows, dim = sequence_input.shape
    layers, shard, wide = w_prev.shape
    tail = DILATIONS[0]
    part = 7 * tail // 4
    edge = (rows - part) // 2
    bf16, f32 = jnp.bfloat16, jnp.float32
    halos, copies = 9, 2 * (shard // TILE)
    anywhere = pl.BlockSpec(memory_space=pl.ANY)
    vmem = pl.BlockSpec(memory_space=pltpu.VMEM)
    block = (rows, dim)
    return pl.pallas_call(
        functools.partial(block_kernel, na, nb, part, edge),
        out_shape=pltpu.VMEM((rows, dim), bf16),
        in_specs=[anywhere, anywhere, anywhere, vmem, anywhere],
        out_specs=vmem,
        scratch_shapes=[
            pltpu.VMEM((layers, na, shard, 2 * wide + dim), bf16),
            pltpu.VMEM(block, bf16),
            pltpu.VMEM((tail, dim), bf16),
            pltpu.VMEM((edge + tail, dim), bf16),
            pltpu.VMEM(block, f32),
            pltpu.VMEM(block, f32),
            pltpu.VMEM(block, bf16),
            pltpu.VMEM(block, bf16),
            pltpu.VMEM(block, bf16),
            pltpu.VMEM(block, bf16),
            pltpu.VMEM(block, bf16),
            pltpu.VMEM(block, bf16),
            pltpu.VMEM((rows, wide), f32),
            pltpu.VMEM((edge, dim), bf16),
            pltpu.SemaphoreType.DMA((layers, 3)),
            pltpu.SemaphoreType.DMA,
            pltpu.SemaphoreType.DMA((layers, copies)),
            pltpu.SemaphoreType.DMA((layers, copies)),
            pltpu.SemaphoreType.DMA((halos,)),
            pltpu.SemaphoreType.DMA((halos,)),
            pltpu.SemaphoreType.REGULAR,
        ],
        compiler_params=pltpu.CompilerParams(
            collective_id=0, has_side_effects=True, vmem_limit_bytes=56 * 2**20
        ),
    )(sequence_input, w_prev, w_now, conv_bias, jnp.swapaxes(w_mix, 1, 2))


def local(na, nb, sequence_input, w_prev, w_now, conv_bias, w_mix):
    rows = sequence_input.shape[0]
    shard = w_prev.shape[1]
    fits = (
        na == 4
        and nb % GROUP == 0
        and shard % TILE == 0
        and shard % (2 * TILE) == 0
        and shard >= 10 * TILE
        and rows % (4 * TILE) == 0
        and rows == 4 * DILATIONS[0]
        and DILATIONS[1] == rows
        and 2 * DILATIONS[2] == nb * rows
    )
    body = functools.partial(kernel_local, na, nb) if fits else plain_local
    return body(sequence_input, w_prev, w_now, conv_bias, w_mix)


def solution(mesh):
    return jax.shard_map(
        functools.partial(local, mesh.shape["seqa"], mesh.shape["seqb"]),
        mesh=mesh,
        in_specs=(
            P(("seqa", "seqb"), None),
            P(None, "seqa", None),
            P(None, "seqa", None),
            P(),
            P(None, None, "seqa"),
        ),
        out_specs=P(("seqa", "seqb"), None),
        check_vma=False,
    )
```

```python
import functools

import jax
import jax.numpy as jnp
from jax import lax
from jax.experimental import pallas as pl
from jax.experimental.pallas import tpu as pltpu
from jax.sharding import PartitionSpec as P

DILATIONS = (128, 512, 2048)
EPS = 1e-06
TILE = 16
GROUP = 4
MESH_ID = pl.DeviceIdType.MESH


def from_behind(value, axis, by):
    peers = lax.axis_size(axis)
    pairs = [(i, i + by) for i in range(peers) if 0 <= i + by < peers]
    return lax.ppermute(value, axis, pairs)


def norm_rows(values):
    scale = lax.rsqrt(jnp.mean(values * values, axis=1, keepdims=True) + EPS)
    return (values * scale).astype(jnp.bfloat16)


def block_prior(normed, dilation_step):
    rows = normed.shape[0]
    whole = dilation_step // rows
    part = dilation_step % rows
    pieces = []
    if part > 0:
        pieces.append(from_behind(normed[rows - part :], ("seqa", "seqb"), whole + 1))
    head = normed[: rows - part]
    if whole > 0:
        head = from_behind(head, ("seqa", "seqb"), whole)
    pieces.append(head)
    return jnp.concatenate(pieces, axis=0)


def one_layer(hidden_state, tap_prev, tap_now, bias, mixing, dilation_step):
    normed = norm_rows(hidden_state)
    earlier = block_prior(normed, dilation_step)
    dim = hidden_state.shape[1]
    pre = bias[None, :] + jnp.dot(
        earlier,
        lax.all_gather(tap_prev, "seqa", axis=0, tiled=True),
        preferred_element_type=jnp.float32,
    )
    pre = pre + jnp.dot(
        normed,
        lax.all_gather(tap_now, "seqa", axis=0, tiled=True),
        preferred_element_type=jnp.float32,
    )
    hidden = (pre[:, :dim] * jax.nn.sigmoid(pre[:, dim:])).astype(jnp.bfloat16)
    return hidden_state + jnp.dot(
        hidden,
        lax.all_gather(mixing, "seqa", axis=1, tiled=True),
        preferred_element_type=jnp.float32,
    )


def plain_local(sequence_input, w_prev, w_now, conv_bias, w_mix):
    state = sequence_input.astype(jnp.float32)
    for layer, step in enumerate(DILATIONS):
        state = one_layer(
            state, w_prev[layer], w_now[layer], conv_bias[layer], w_mix[layer], step
        )
    return state.astype(jnp.bfloat16)


def flip(value, bit):
    return value + bit - 2 * bit * ((value // bit) % 2)


def block_kernel(
    na, nb, part, edge,
    x_hbm, wp_hbm, wn_hbm, bias_ref, wm_hbm,
    out_ref,
    w, xin, xt, xp, state1, state2, u0, h0, u1, h1, u2, h2, pre, oback,
    load_sem, x_sem, send, recv, halo_send, halo_recv, hello,
):
    layers, dim = wp_hbm.shape[0], x_hbm.shape[1]
    wide = 2 * dim
    shard = wp_hbm.shape[1]
    rows = x_hbm.shape[0]
    n = na * nb
    tail = DILATIONS[0]
    window = edge + tail
    lead_rows = edge + part
    f32, bf16 = jnp.float32, jnp.bfloat16
    a, b = lax.axis_index("seqa"), lax.axis_index("seqb")
    me = a * nb + b
    a1, a2 = flip(a, 1), flip(a, 2)
    b1, b2 = flip(b, 1), flip(b, 2)
    tiles = shard // TILE
    zs = tiles // 5
    ys = tiles // 2 - zs
    yb, zb = b % 2, b // 2 % 2
    shares = [(ys, zs, None), (ys - 2, zs, None), (ys - 1, zs - 1, None)]

    def at(index):
        return (index // nb, index % nb)

    hop = DILATIONS[2] // rows
    half, q = b // hop, b % hop
    other = 1 - half
    pair = (a, (b + hop) % nb)
    wrap = (q + 1) // hop
    next_b = half * hop + (q + 1) % hop
    last_b = half * hop + (q + hop - 1) % hop
    after_a, before_a = (a + 1) % na, (a + na - 1) % na
    up, down = a + 1 < na, a > 0
    has_next, has_last = me + 1 < n, me > 0
    has_far, had_far = me + hop < n, me >= hop
    lead = jnp.where(q == 0, other, half)

    def place1(s):
        return pl.multiple_of(jnp.where(s == lead, 0, lead_rows), TILE)

    def place2(s):
        return pl.multiple_of(jnp.where(s == half, 0, lead_rows), TILE)

    loads = []
    for l in range(layers):
        loads.append([
            pltpu.make_async_copy(wp_hbm.at[l], w.at[l, a, :, pl.ds(0, wide)], load_sem.at[l, 0]),
            pltpu.make_async_copy(wn_hbm.at[l], w.at[l, a, :, pl.ds(wide, wide)], load_sem.at[l, 1]),
            pltpu.make_async_copy(wm_hbm.at[l], w.at[l, a, :, pl.ds(2 * wide, dim)], load_sem.at[l, 2]),
        ])
    for c in loads[0]:
        c.start()
    x_load = pltpu.make_async_copy(x_hbm, xin, x_sem)
    x_load.start()
    for l in range(1, layers):
        for c in loads[l]:
            c.start()

    z = b // 2
    inner = jnp.logical_and(z > 0, z < nb // 2 - 1)
    beside = (a, (b + nb - 2 + 4 * (z % 2)) % nb)

    def greet(sem, more):
        count = 4
        for dev in ((a1, b), (a2, b), (a, b1), (a, b2)):
            pl.semaphore_signal(sem, inc=1, device_id=dev, device_id_type=MESH_ID)
        for to, dev, come in [(inner, beside, inner)] + more:
            @pl.when(to)
            def _(dev=dev):
                pl.semaphore_signal(sem, inc=1, device_id=dev, device_id_type=MESH_ID)

            count = count + come.astype(jnp.int32)
        pl.semaphore_wait(sem, count)

    both = jnp.logical_and
    greet(pltpu.get_barrier_semaphore(), [
        (both(b == 0, down), (before_a, nb - 1), both(b == nb - 1, up)),
        (half == 0, pair, half == 1),
        (both(half == 0, down), (before_a, (b + hop) % nb), both(half == 1, up)),
        (q == 0, (a, last_b), wrap == 1),
        (both(q == 0, down), (before_a, last_b), both(wrap == 1, up)),
    ])

    def move(l, k, owner, start, size, dev):
        ref = w.at[l, owner, pl.ds(pl.multiple_of(start * TILE, TILE), size * TILE)]
        return pltpu.make_async_remote_copy(
            src_ref=ref, dst_ref=ref, send_sem=send.at[l, k], recv_sem=recv.at[l, k],
            device_id=dev, device_id_type=MESH_ID,
        )

    core, across, ynear, znear = (a1, b), (a2, b), (a, b1), (a, b2)
    moves, orders, lasts, sent = [], [], [], []
    fours, rest4 = tiles // 5, tiles - tiles // 5 * 4
    p = b % GROUP
    py, pz = flip(p, 1), flip(p, 2)
    pyz = flip(py, 2)
    plan = [(across, p, i) for i in range(fours)] + [(across, GROUP, i) for i in range(rest4)]
    plan += [(ynear, p, i) for i in range(fours)] + [(znear, p, i) for i in range(fours)]
    plan += [(ynear, pz, i) for i in range(fours)]
    x_own, x_rest, y_own, z_own, y_hop, plain = (
        0, fours, fours + rest4, 2 * fours + rest4, 3 * fours + rest4, 4 * fours + rest4
    )
    here = [
        move(0, k, a if dev is across else a2, block * fours + i, 1, dev)
        for k, (dev, block, i) in enumerate(plan)
    ]
    here.append(move(0, plain, a, 0, tiles, core))
    for k, (block, size) in enumerate(
        [(p, fours), (GROUP, rest4), (py, fours), (pz, fours), (pyz, fours)]
    ):
        here.append(move(0, plain + 1 + k, a2, block * fours, size, core))
    moves.append(here)
    sent += [(m, None) for m in here]
    orders.append(([(2, 0)] * (fours + rest4), None, None, None, None, None))
    lasts.append(plain)

    def arrive(k, then=()):
        moves[0][k].wait_recv()
        for t in then:
            moves[0][t].start()

    def layer0_own():
        for i in range(fours):
            arrive(x_own + i, (y_own + i, z_own + i))
        moves[0][plain + 1].start()

    def layer0_rest():
        for i in range(max(fours, rest4)):
            if i < rest4:
                arrive(x_rest + i)
            if i < fours:
                arrive(z_own + i, (y_hop + i,))
        moves[0][plain + 2].start()
        moves[0][plain + 4].start()
        for i in range(fours):
            arrive(y_own + i)
        moves[0][plain + 3].start()

    def layer0_hops():
        for i in range(fours):
            arrive(y_hop + i)
        moves[0][plain + 5].start()

    for l, (y, z, spread) in enumerate(shares[1:], 1):
        pick = 0 if spread is None else 1
        rest = tiles - 2 * (y + z + pick)
        swap = 2 * (y + z)
        own = (yb * y, 2 * y + zb * z, swap + 2 * pick, swap + zb, swap + 1 - zb)
        theirs = ((1 - yb) * y, 2 * y + (1 - zb) * z)
        sizes = (y, z, rest, pick, pick)
        order = [(1, i) for i in range(z)] + [(3, i) for i in range(pick)]
        order += [(0, i) for i in range(y)] + [(2, i) for i in range(rest)] + [(4, i) for i in range(pick)]
        mine = spread and spread(a // 2, yb)
        away = spread and jnp.logical_not(spread(1 - a // 2, yb))
        here = [(move(l, k, a, own[f] + i, 1, across), away if f == 4 else None) for k, (f, i) in enumerate(order)]
        relays = {}
        for k, (f, i) in enumerate(order):
            if f in (0, 1, 3):
                relays[k] = len(here)
                here.append((
                    move(l, len(here), a2, own[f] + i, 1, znear if f else ynear), mine if f == 3 else None
                ))
        last = len(here)
        here.append((move(l, last, a, 0, tiles, core), None))
        local = {}
        for f in range(5):
            if sizes[f]:
                local[f] = len(here)
                here.append((move(l, len(here), a2, own[f], sizes[f], core), None))
        for f in range(2):
            here.append((move(l, len(here), a2, theirs[f], sizes[f], core), None))
        moves.append([m for m, _ in here])
        sent += here
        orders.append((order, sizes, relays, local, mine, away))
        lasts.append(last)

    def maybe(there, do):
        if there is None:
            do()
        else:
            pl.when(there)(do)

    def start_weights(l):
        order, away = orders[l][0], orders[l][5]
        for k, (f, _) in enumerate(order):
            maybe(away if f == 4 else None, moves[l][k].start)
        moves[l][lasts[l]].start()

    def relay(l, k):
        order, sizes, relays, local, mine, _ = orders[l]
        f, i = order[k]

        def here():
            moves[l][k].wait_recv()
            if k in relays:
                maybe(mine if f == 3 else None, moves[l][relays[k]].start)
            if i == sizes[f] - 1:
                moves[l][local[f]].start()

        maybe(jnp.logical_not(mine) if f == 4 else None, here)

    def gather(l, f):
        order, sizes, relays, local, mine, _ = orders[l]
        for k in relays:
            if order[k][0] == f:
                moves[l][relays[k]].wait_recv()
        moves[l][len(moves[l]) - 2 + f].start()
        for k in relays:
            if f == 1 and order[k][0] == 3:
                @pl.when(mine)
                def _(k=k):
                    moves[l][relays[k]].wait_recv()
                    moves[l][local[4]].start()

    def finish(l):
        for k in range(lasts[l], len(moves[l])):
            moves[l][k].wait_recv()

    def halo(src, dst, slot, dev):
        return pltpu.make_async_remote_copy(
            src_ref=src, dst_ref=dst, send_sem=halo_send.at[slot], recv_sem=halo_recv.at[slot],
            device_id=dev, device_id_type=MESH_ID,
        )

    mine = pl.ds(edge, part)
    x_next = halo(xin.at[pl.ds(rows - tail, tail)], xt, 0, at((me + 1) % n))
    cut = window // TILE // 2 * TILE
    x_pair = [
        halo(
            xin.at[pl.ds(pl.multiple_of(part - tail + other * edge + lo, TILE), size)],
            xp.at[pl.ds(lo, size)], slot, pair,
        )
        for lo, size, slot in ((0, cut, 1), (cut, window - cut, 8))
    ]
    second_home = halo(u1.at[mine], h1.at[mine], 2, at((me + 1) % n))

    def second(s):
        to = s + wrap
        slot = to % 2
        return halo(
            u1.at[pl.ds(place1(s), edge)], h1.at[pl.ds(place1_at_next(slot), edge)],
            3 + slot, ((a + to // 2) % na, next_b),
        ), a + to // 2 < na

    def place1_at_next(slot):
        first = jnp.where(wrap == 1, other, half)
        return pl.multiple_of(jnp.where(slot == first, 0, lead_rows), TILE)

    third_home = halo(u2.at[mine], h2.at[mine], 5, at((me + hop) % n))
    third = halo(u2.at[pl.ds(place2(1), edge)], h2.at[pl.ds(place2(0), edge)], 6, (after_a, b))
    edge_rows = pl.ds(pl.multiple_of(part + half * edge, TILE), edge)
    back = halo(oback, out_ref.at[edge_rows], 7, pair)
    near_cut = (b // 2) % 2 != half

    for c in loads[0]:
        c.wait()
    start_weights(0)
    x_load.wait()
    greet(hello, [])
    pl.when(has_next)(x_next.start)

    def pair_rest():
        pl.when(jnp.logical_not(near_cut))(x_pair[0].start)
        pl.when(jnp.logical_not(near_cut))(x_pair[1].start)

    pl.when(near_cut)(x_pair[0].start)
    pl.when(near_cut)(x_pair[1].start)
    for l in range(1, layers):
        for c in loads[l]:
            c.wait()
        start_weights(l)

    @pl.when(me == 0)
    def _():
        xt[...] = jnp.zeros(xt.shape, xt.dtype)
        h1[mine] = jnp.zeros((part, dim), h1.dtype)

    @pl.when(both(a == 0, q == 0))
    def _():
        h1[pl.ds(place1(0), edge)] = jnp.zeros((edge, dim), h1.dtype)

    @pl.when(a == 0)
    def _():
        h2[pl.ds(place2(0), edge)] = jnp.zeros((edge, dim), h2.dtype)

    @pl.when(jnp.logical_not(had_far))
    def _():
        h2[mine] = jnp.zeros((part, dim), h2.dtype)

    def enter(ref, start, lo):
        normed = norm_rows(ref[pl.ds(start, window)].astype(f32))
        h0[lo : lo + edge] = normed[:edge]
        u0[lo : lo + edge] = normed[tail:]

    def tap(l, lo):
        return w[l, :, :, lo : lo + wide].reshape(na * shard, wide)

    front, rear = (0, lead_rows), (lead_rows, edge)
    lead_span, home_span = (0, edge), (edge, part)

    def now_part(l, now, span):
        lo, size = span
        pre[lo : lo + size] = bias_ref[l : l + 1, :] + jnp.dot(
            now[lo : lo + size], tap(l, wide), preferred_element_type=f32
        )

    def rest_part(l, earlier, span):
        lo, size = span
        total = pre[lo : lo + size] + jnp.dot(
            earlier[lo : lo + size], tap(l, 0), preferred_element_type=f32
        )
        hidden = (total[:, :dim] * jax.nn.sigmoid(total[:, dim:])).astype(bf16)
        mix = w[l, :, :, 2 * wide :].reshape(na * shard, dim)
        return lax.dot_general(hidden, mix, (((1,), (1,)), ((), ())), preferred_element_type=f32)

    enter(xin, pl.multiple_of(part - tail + half * edge, TILE), 0)
    home = norm_rows(xin[:part].astype(f32))
    u0[mine] = home
    if part > tail:
        h0[edge + tail : lead_rows] = home[: part - tail]
    layer0_own()
    pair_rest()
    layer0_rest()
    relay(1, 0)
    layer0_hops()
    pl.when(has_last)(x_next.wait_recv)
    h0[edge : edge + tail] = norm_rows(xt[...].astype(f32))
    relay(1, 1)
    finish(0)

    def leave1(new, spot):
        state1[spot] = new
        u1[spot] = norm_rows(new)

    now_part(0, u0, front)
    relay(1, 2)
    grown = rest_part(0, h0, front)
    own_start = pl.multiple_of(part + half * edge, TILE)
    leave1(xin[pl.ds(own_start, edge)].astype(f32) + grown[:edge], pl.ds(place1(half), edge))
    leave1(xin[:part].astype(f32) + grown[edge:], mine)
    pl.when(has_next)(second_home.start)
    copy, there = second(half)
    pl.when(there)(copy.start)
    for c in x_pair:
        c.wait_recv()
    enter(xp, 0, lead_rows)
    now_part(0, u0, rear)
    relay(1, 3)
    grown = rest_part(0, h0, rear)
    leave1(xp[tail:].astype(f32) + grown, pl.ds(place1(other), edge))
    copy, there = second(other)
    pl.when(there)(copy.start)
    for k in range(4, len(orders[1][0])):
        relay(1, k)
    gather(1, 1)
    gather(1, 0)
    finish(1)
    now_part(1, u1, front)
    now_part(1, u1, rear)
    relay(2, 0)

    def takes(s):
        @pl.when(jnp.logical_or(q + s > 0, down))
        def _():
            spot = pl.ds(place1(s), edge)
            halo(u1.at[spot], h1.at[spot], 3 + s, pair).wait_recv()

    def leave2(new, spot):
        normed = norm_rows(new)
        state2[spot] = new
        u2[spot] = normed
        return normed

    def leave2_edge(new, s):
        normed = leave2(new, pl.ds(place2(s), edge))

        @pl.when(s == 0)
        def _():
            h2[pl.ds(place2(1), edge)] = normed

        @pl.when(both(s == 1, up))
        def _():
            third.start()

    pl.when(has_last)(second_home.wait_recv)
    leave2(state1[mine] + rest_part(1, h1, home_span), mine)
    pl.when(has_far)(third_home.start)
    relay(2, 1)
    def middle():
        relay(2, 2)

    pl.when(b % 2 == 0)(middle)
    takes(lead)
    leave2_edge(state1[:edge] + rest_part(1, h1, lead_span), lead)
    pl.when(jnp.logical_not(b % 2 == 0))(middle)
    relay(2, 3)

    def last_relays():
        for k in range(4, len(orders[2][0])):
            relay(2, k)
        gather(2, 1)
        gather(2, 0)

    pl.when(b % 2 == 0)(last_relays)

    takes(1 - lead)
    leave2_edge(state1[lead_rows:] + rest_part(1, h1, rear), 1 - lead)
    pl.when(b % 2 == 1)(last_relays)
    finish(2)

    def takes_third(s):
        @pl.when(both(s == 0, down))
        def _():
            third.wait_recv()

    def end_rear():
        now_part(2, u2, rear)
        takes_third(other)
        oback[...] = (state2[lead_rows:] + rest_part(2, h2, rear)).astype(bf16)
        back.start()

    def end_front():
        now_part(2, u2, front)
        takes_third(half)
        out_ref[edge_rows] = (state2[:edge] + rest_part(2, h2, lead_span)).astype(bf16)
        pl.when(had_far)(third_home.wait_recv)
        out_ref[:part] = (state2[mine] + rest_part(2, h2, home_span)).astype(bf16)

    early = jnp.logical_or(near_cut, both(half == 0, a >= na // 2) | both(half == 1, a >= na // 2))
    pl.when(early)(end_rear)
    end_front()
    pl.when(jnp.logical_not(early))(end_rear)
    for m, there in sent:
        maybe(there, m.wait_send)
    for s in range(2):
        copy, there = second(s)
        pl.when(there)(copy.wait_send)
    pl.when(has_next)(second_home.wait_send)
    pl.when(has_next)(x_next.wait_send)
    pl.when(has_far)(third_home.wait_send)
    pl.when(up)(third.wait_send)
    for c in x_pair:
        c.wait_send()
    back.wait_send()
    back.wait_recv()


def kernel_local(na, nb, sequence_input, w_prev, w_now, conv_bias, w_mix):
    rows, dim = sequence_input.shape
    layers, shard, wide = w_prev.shape
    tail = DILATIONS[0]
    part = 7 * tail // 4
    edge = (rows - part) // 2
    bf16, f32 = jnp.bfloat16, jnp.float32
    halos, copies = 9, 2 * (shard // TILE)
    anywhere = pl.BlockSpec(memory_space=pl.ANY)
    vmem = pl.BlockSpec(memory_space=pltpu.VMEM)
    block = (rows, dim)
    return pl.pallas_call(
        functools.partial(block_kernel, na, nb, part, edge),
        out_shape=pltpu.VMEM((rows, dim), bf16),
        in_specs=[anywhere, anywhere, anywhere, vmem, anywhere],
        out_specs=vmem,
        scratch_shapes=[
            pltpu.VMEM((layers, na, shard, 2 * wide + dim), bf16),
            pltpu.VMEM(block, bf16),
            pltpu.VMEM((tail, dim), bf16),
            pltpu.VMEM((edge + tail, dim), bf16),
            pltpu.VMEM(block, f32),
            pltpu.VMEM(block, f32),
            pltpu.VMEM(block, bf16),
            pltpu.VMEM(block, bf16),
            pltpu.VMEM(block, bf16),
            pltpu.VMEM(block, bf16),
            pltpu.VMEM(block, bf16),
            pltpu.VMEM(block, bf16),
            pltpu.VMEM((rows, wide), f32),
            pltpu.VMEM((edge, dim), bf16),
            pltpu.SemaphoreType.DMA((layers, 3)),
            pltpu.SemaphoreType.DMA,
            pltpu.SemaphoreType.DMA((layers, copies)),
            pltpu.SemaphoreType.DMA((layers, copies)),
            pltpu.SemaphoreType.DMA((halos,)),
            pltpu.SemaphoreType.DMA((halos,)),
            pltpu.SemaphoreType.REGULAR,
        ],
        compiler_params=pltpu.CompilerParams(
            collective_id=0, has_side_effects=True, vmem_limit_bytes=56 * 2**20
        ),
    )(sequence_input, w_prev, w_now, conv_bias, jnp.swapaxes(w_mix, 1, 2))


def local(na, nb, sequence_input, w_prev, w_now, conv_bias, w_mix):
    rows = sequence_input.shape[0]
    shard = w_prev.shape[1]
    fits = (
        na == 4
        and nb % GROUP == 0
        and shard % TILE == 0
        and shard % (2 * TILE) == 0
        and shard >= 10 * TILE
        and rows % (4 * TILE) == 0
        and rows == 4 * DILATIONS[0]
        and DILATIONS[1] == rows
        and 2 * DILATIONS[2] == nb * rows
    )
    body = functools.partial(kernel_local, na, nb) if fits else plain_local
    return body(sequence_input, w_prev, w_now, conv_bias, w_mix)


def solution(mesh):
    return jax.shard_map(
        functools.partial(local, mesh.shape["seqa"], mesh.shape["seqb"]),
        mesh=mesh,
        in_specs=(
            P(("seqa", "seqb"), None),
            P(None, "seqa", None),
            P(None, "seqa", None),
            P(),
            P(None, None, "seqa"),
        ),
        out_specs=P(("seqa", "seqb"), None),
        check_vma=False,
    )
```

```python
import functools

import jax
import jax.numpy as jnp
from jax import lax
from jax.experimental import pallas as pl
from jax.experimental.pallas import tpu as pltpu
from jax.sharding import PartitionSpec as P

DILATIONS = (128, 512, 2048)
EPS = 1e-06
TILE = 16
GROUP = 4
MESH_ID = pl.DeviceIdType.MESH


def from_behind(value, axis, by):
    peers = lax.axis_size(axis)
    pairs = [(i, i + by) for i in range(peers) if 0 <= i + by < peers]
    return lax.ppermute(value, axis, pairs)


def norm_rows(values):
    scale = lax.rsqrt(jnp.mean(values * values, axis=1, keepdims=True) + EPS)
    return (values * scale).astype(jnp.bfloat16)


def block_prior(normed, dilation_step):
    rows = normed.shape[0]
    whole = dilation_step // rows
    part = dilation_step % rows
    pieces = []
    if part > 0:
        pieces.append(from_behind(normed[rows - part :], ("seqa", "seqb"), whole + 1))
    head = normed[: rows - part]
    if whole > 0:
        head = from_behind(head, ("seqa", "seqb"), whole)
    pieces.append(head)
    return jnp.concatenate(pieces, axis=0)


def one_layer(hidden_state, tap_prev, tap_now, bias, mixing, dilation_step):
    normed = norm_rows(hidden_state)
    earlier = block_prior(normed, dilation_step)
    dim = hidden_state.shape[1]
    pre = bias[None, :] + jnp.dot(
        earlier,
        lax.all_gather(tap_prev, "seqa", axis=0, tiled=True),
        preferred_element_type=jnp.float32,
    )
    pre = pre + jnp.dot(
        normed,
        lax.all_gather(tap_now, "seqa", axis=0, tiled=True),
        preferred_element_type=jnp.float32,
    )
    hidden = (pre[:, :dim] * jax.nn.sigmoid(pre[:, dim:])).astype(jnp.bfloat16)
    return hidden_state + jnp.dot(
        hidden,
        lax.all_gather(mixing, "seqa", axis=1, tiled=True),
        preferred_element_type=jnp.float32,
    )


def plain_local(sequence_input, w_prev, w_now, conv_bias, w_mix):
    state = sequence_input.astype(jnp.float32)
    for layer, step in enumerate(DILATIONS):
        state = one_layer(
            state, w_prev[layer], w_now[layer], conv_bias[layer], w_mix[layer], step
        )
    return state.astype(jnp.bfloat16)


def flip(value, bit):
    return value + bit - 2 * bit * ((value // bit) % 2)


def block_kernel(
    na, nb, part, edge,
    x_hbm, wp_hbm, wn_hbm, bias_ref, wm_hbm,
    out_ref,
    w, xin, xt, xp, state1, state2, u0, h0, u1, h1, u2, h2, pre, oback,
    load_sem, x_sem, send, recv, halo_send, halo_recv, hello,
):
    layers, dim = wp_hbm.shape[0], x_hbm.shape[1]
    wide = 2 * dim
    shard = wp_hbm.shape[1]
    rows = x_hbm.shape[0]
    n = na * nb
    tail = DILATIONS[0]
    window = edge + tail
    lead_rows = edge + part
    f32, bf16 = jnp.float32, jnp.bfloat16
    a, b = lax.axis_index("seqa"), lax.axis_index("seqb")
    me = a * nb + b
    a1, a2 = flip(a, 1), flip(a, 2)
    b1, b2 = flip(b, 1), flip(b, 2)
    tiles = shard // TILE
    zs = tiles // 5
    ys = tiles // 2 - zs
    yb, zb = b % 2, b // 2 % 2
    shares = [(ys, zs, None), (ys - 2, zs, None), (ys - 1, zs - 1, None)]

    def at(index):
        return (index // nb, index % nb)

    hop = DILATIONS[2] // rows
    half, q = b // hop, b % hop
    other = 1 - half
    pair = (a, (b + hop) % nb)
    wrap = (q + 1) // hop
    next_b = half * hop + (q + 1) % hop
    last_b = half * hop + (q + hop - 1) % hop
    after_a, before_a = (a + 1) % na, (a + na - 1) % na
    up, down = a + 1 < na, a > 0
    has_next, has_last = me + 1 < n, me > 0
    has_far, had_far = me + hop < n, me >= hop
    lead = jnp.where(q == 0, other, half)

    def place1(s):
        return pl.multiple_of(jnp.where(s == lead, 0, lead_rows), TILE)

    def place2(s):
        return pl.multiple_of(jnp.where(s == half, 0, lead_rows), TILE)

    loads = []
    for l in range(layers):
        loads.append([
            pltpu.make_async_copy(wp_hbm.at[l], w.at[l, a, :, pl.ds(0, wide)], load_sem.at[l, 0]),
            pltpu.make_async_copy(wn_hbm.at[l], w.at[l, a, :, pl.ds(wide, wide)], load_sem.at[l, 1]),
            pltpu.make_async_copy(wm_hbm.at[l], w.at[l, a, :, pl.ds(2 * wide, dim)], load_sem.at[l, 2]),
        ])
    for c in loads[0]:
        c.start()
    x_load = pltpu.make_async_copy(x_hbm, xin, x_sem)
    x_load.start()
    for l in range(1, layers):
        for c in loads[l]:
            c.start()

    z = b // 2
    inner = jnp.logical_and(z > 0, z < nb // 2 - 1)
    beside = (a, (b + nb - 2 + 4 * (z % 2)) % nb)

    def greet(sem, more):
        count = 4
        for dev in ((a1, b), (a2, b), (a, b1), (a, b2)):
            pl.semaphore_signal(sem, inc=1, device_id=dev, device_id_type=MESH_ID)
        for to, dev, come in [(inner, beside, inner)] + more:
            @pl.when(to)
            def _(dev=dev):
                pl.semaphore_signal(sem, inc=1, device_id=dev, device_id_type=MESH_ID)

            count = count + come.astype(jnp.int32)
        pl.semaphore_wait(sem, count)

    both = jnp.logical_and
    greet(pltpu.get_barrier_semaphore(), [
        (both(b == 0, down), (before_a, nb - 1), both(b == nb - 1, up)),
        (half == 0, pair, half == 1),
        (both(half == 0, down), (before_a, (b + hop) % nb), both(half == 1, up)),
        (q == 0, (a, last_b), wrap == 1),
        (both(q == 0, down), (before_a, last_b), both(wrap == 1, up)),
    ])

    def move(l, k, owner, start, size, dev):
        ref = w.at[l, owner, pl.ds(pl.multiple_of(start * TILE, TILE), size * TILE)]
        return pltpu.make_async_remote_copy(
            src_ref=ref, dst_ref=ref, send_sem=send.at[l, k], recv_sem=recv.at[l, k],
            device_id=dev, device_id_type=MESH_ID,
        )

    core, across, ynear, znear = (a1, b), (a2, b), (a, b1), (a, b2)
    moves, orders, lasts, sent = [], [], [], []
    fours, rest4 = tiles // 5, tiles - tiles // 5 * 4
    p = b % GROUP
    py, pz = flip(p, 1), flip(p, 2)
    pyz = flip(py, 2)
    plan = [(across, p, i) for i in range(fours)] + [(across, GROUP, i) for i in range(rest4)]
    plan += [(ynear, p, i) for i in range(fours)] + [(znear, p, i) for i in range(fours)]
    plan += [(ynear, pz, i) for i in range(fours)]
    x_own, x_rest, y_own, z_own, y_hop, plain = (
        0, fours, fours + rest4, 2 * fours + rest4, 3 * fours + rest4, 4 * fours + rest4
    )
    here = [
        move(0, k, a if dev is across else a2, block * fours + i, 1, dev)
        for k, (dev, block, i) in enumerate(plan)
    ]
    here.append(move(0, plain, a, 0, tiles, core))
    for k, (block, size) in enumerate(
        [(p, fours), (GROUP, rest4), (py, fours), (pz, fours), (pyz, fours)]
    ):
        here.append(move(0, plain + 1 + k, a2, block * fours, size, core))
    moves.append(here)
    sent += [(m, None) for m in here]
    orders.append(([(2, 0)] * (fours + rest4), None, None, None, None, None))
    lasts.append(plain)

    def arrive(k, then=()):
        moves[0][k].wait_recv()
        for t in then:
            moves[0][t].start()

    def layer0_own():
        for i in range(fours):
            arrive(x_own + i, (y_own + i, z_own + i))
        moves[0][plain + 1].start()

    def layer0_rest():
        for i in range(max(fours, rest4)):
            if i < rest4:
                arrive(x_rest + i)
            if i < fours:
                arrive(z_own + i, (y_hop + i,))
        moves[0][plain + 2].start()
        moves[0][plain + 4].start()
        for i in range(fours):
            arrive(y_own + i)
        moves[0][plain + 3].start()

    def layer0_hops():
        for i in range(fours):
            arrive(y_hop + i)
        moves[0][plain + 5].start()

    for l, (y, z, spread) in enumerate(shares[1:], 1):
        pick = 0 if spread is None else 1
        rest = tiles - 2 * (y + z + pick)
        swap = 2 * (y + z)
        own = (yb * y, 2 * y + zb * z, swap + 2 * pick, swap + zb, swap + 1 - zb)
        theirs = ((1 - yb) * y, 2 * y + (1 - zb) * z)
        sizes = (y, z, rest, pick, pick)
        order = [(1, i) for i in range(z)] + [(3, i) for i in range(pick)]
        order += [(0, i) for i in range(y)] + [(2, i) for i in range(rest)] + [(4, i) for i in range(pick)]
        mine = spread and spread(a // 2, yb)
        away = spread and jnp.logical_not(spread(1 - a // 2, yb))
        here = [(move(l, k, a, own[f] + i, 1, across), away if f == 4 else None) for k, (f, i) in enumerate(order)]
        relays = {}
        for k, (f, i) in enumerate(order):
            if f in (0, 1, 3):
                relays[k] = len(here)
                here.append((
                    move(l, len(here), a2, own[f] + i, 1, znear if f else ynear), mine if f == 3 else None
                ))
        last = len(here)
        here.append((move(l, last, a, 0, tiles, core), None))
        local = {}
        for f in range(5):
            if sizes[f]:
                local[f] = len(here)
                here.append((move(l, len(here), a2, own[f], sizes[f], core), None))
        for f in range(2):
            here.append((move(l, len(here), a2, theirs[f], sizes[f], core), None))
        moves.append([m for m, _ in here])
        sent += here
        orders.append((order, sizes, relays, local, mine, away))
        lasts.append(last)

    def maybe(there, do):
        if there is None:
            do()
        else:
            pl.when(there)(do)

    def start_weights(l):
        order, away = orders[l][0], orders[l][5]
        for k, (f, _) in enumerate(order):
            maybe(away if f == 4 else None, moves[l][k].start)
        moves[l][lasts[l]].start()

    def relay(l, k):
        order, sizes, relays, local, mine, _ = orders[l]
        f, i = order[k]

        def here():
            moves[l][k].wait_recv()
            if k in relays:
                maybe(mine if f == 3 else None, moves[l][relays[k]].start)
            if i == sizes[f] - 1:
                moves[l][local[f]].start()

        maybe(jnp.logical_not(mine) if f == 4 else None, here)

    def gather(l, f):
        order, sizes, relays, local, mine, _ = orders[l]
        for k in relays:
            if order[k][0] == f:
                moves[l][relays[k]].wait_recv()
        moves[l][len(moves[l]) - 2 + f].start()
        for k in relays:
            if f == 1 and order[k][0] == 3:
                @pl.when(mine)
                def _(k=k):
                    moves[l][relays[k]].wait_recv()
                    moves[l][local[4]].start()

    def finish(l):
        for k in range(lasts[l], len(moves[l])):
            moves[l][k].wait_recv()

    def halo(src, dst, slot, dev):
        return pltpu.make_async_remote_copy(
            src_ref=src, dst_ref=dst, send_sem=halo_send.at[slot], recv_sem=halo_recv.at[slot],
            device_id=dev, device_id_type=MESH_ID,
        )

    mine = pl.ds(edge, part)
    x_next = halo(xin.at[pl.ds(rows - tail, tail)], xt, 0, at((me + 1) % n))
    cut = window // TILE // 2 * TILE
    x_pair = [
        halo(
            xin.at[pl.ds(pl.multiple_of(part - tail + other * edge + lo, TILE), size)],
            xp.at[pl.ds(lo, size)], slot, pair,
        )
        for lo, size, slot in ((0, cut, 1), (cut, window - cut, 8))
    ]
    second_home = halo(u1.at[mine], h1.at[mine], 2, at((me + 1) % n))

    def second(s):
        to = s + wrap
        slot = to % 2
        return halo(
            u1.at[pl.ds(place1(s), edge)], h1.at[pl.ds(place1_at_next(slot), edge)],
            3 + slot, ((a + to // 2) % na, next_b),
        ), a + to // 2 < na

    def place1_at_next(slot):
        first = jnp.where(wrap == 1, other, half)
        return pl.multiple_of(jnp.where(slot == first, 0, lead_rows), TILE)

    third_home = halo(u2.at[mine], h2.at[mine], 5, at((me + hop) % n))
    third = halo(u2.at[pl.ds(place2(1), edge)], h2.at[pl.ds(place2(0), edge)], 6, (after_a, b))
    edge_rows = pl.ds(pl.multiple_of(part + half * edge, TILE), edge)
    back = halo(oback, out_ref.at[edge_rows], 7, pair)
    near_cut = (b // 2) % 2 != half

    for c in loads[0]:
        c.wait()
    start_weights(0)
    x_load.wait()
    greet(hello, [])
    pl.when(has_next)(x_next.start)

    def pair_rest():
        pl.when(jnp.logical_not(near_cut))(x_pair[0].start)
        pl.when(jnp.logical_not(near_cut))(x_pair[1].start)

    pl.when(near_cut)(x_pair[0].start)
    pl.when(near_cut)(x_pair[1].start)
    for l in range(1, layers):
        for c in loads[l]:
            c.wait()
        start_weights(l)

    @pl.when(me == 0)
    def _():
        xt[...] = jnp.zeros(xt.shape, xt.dtype)
        h1[mine] = jnp.zeros((part, dim), h1.dtype)

    @pl.when(both(a == 0, q == 0))
    def _():
        h1[pl.ds(place1(0), edge)] = jnp.zeros((edge, dim), h1.dtype)

    @pl.when(a == 0)
    def _():
        h2[pl.ds(place2(0), edge)] = jnp.zeros((edge, dim), h2.dtype)

    @pl.when(jnp.logical_not(had_far))
    def _():
        h2[mine] = jnp.zeros((part, dim), h2.dtype)

    def enter(ref, start, lo):
        normed = norm_rows(ref[pl.ds(start, window)].astype(f32))
        h0[lo : lo + edge] = normed[:edge]
        u0[lo : lo + edge] = normed[tail:]

    def tap(l, lo):
        return w[l, :, :, lo : lo + wide].reshape(na * shard, wide)

    front, rear = (0, lead_rows), (lead_rows, edge)
    lead_span, home_span = (0, edge), (edge, part)

    def now_part(l, now, span):
        lo, size = span
        pre[lo : lo + size] = bias_ref[l : l + 1, :] + jnp.dot(
            now[lo : lo + size], tap(l, wide), preferred_element_type=f32
        )

    def rest_part(l, earlier, span):
        lo, size = span
        total = pre[lo : lo + size] + jnp.dot(
            earlier[lo : lo + size], tap(l, 0), preferred_element_type=f32
        )
        hidden = (total[:, :dim] * jax.nn.sigmoid(total[:, dim:])).astype(bf16)
        mix = w[l, :, :, 2 * wide :].reshape(na * shard, dim)
        return lax.dot_general(hidden, mix, (((1,), (1,)), ((), ())), preferred_element_type=f32)

    enter(xin, pl.multiple_of(part - tail + half * edge, TILE), 0)
    home = norm_rows(xin[:part].astype(f32))
    u0[mine] = home
    if part > tail:
        h0[edge + tail : lead_rows] = home[: part - tail]
    layer0_own()
    pair_rest()
    layer0_rest()
    relay(1, 0)
    layer0_hops()
    pl.when(has_last)(x_next.wait_recv)
    h0[edge : edge + tail] = norm_rows(xt[...].astype(f32))
    relay(1, 1)
    finish(0)

    def leave1(new, spot):
        state1[spot] = new
        u1[spot] = norm_rows(new)

    now_part(0, u0, front)
    relay(1, 2)
    grown = rest_part(0, h0, front)
    own_start = pl.multiple_of(part + half * edge, TILE)
    leave1(xin[pl.ds(own_start, edge)].astype(f32) + grown[:edge], pl.ds(place1(half), edge))
    leave1(xin[:part].astype(f32) + grown[edge:], mine)
    pl.when(has_next)(second_home.start)
    copy, there = second(half)
    pl.when(there)(copy.start)
    for c in x_pair:
        c.wait_recv()
    enter(xp, 0, lead_rows)
    now_part(0, u0, rear)
    relay(1, 3)
    grown = rest_part(0, h0, rear)
    leave1(xp[tail:].astype(f32) + grown, pl.ds(place1(other), edge))
    copy, there = second(other)
    pl.when(there)(copy.start)
    for k in range(4, len(orders[1][0])):
        relay(1, k)
    gather(1, 1)
    gather(1, 0)
    finish(1)
    now_part(1, u1, front)
    now_part(1, u1, rear)
    relay(2, 0)

    def takes(s):
        @pl.when(jnp.logical_or(q + s > 0, down))
        def _():
            spot = pl.ds(place1(s), edge)
            halo(u1.at[spot], h1.at[spot], 3 + s, pair).wait_recv()

    def leave2(new, spot):
        normed = norm_rows(new)
        state2[spot] = new
        u2[spot] = normed
        return normed

    def leave2_edge(new, s):
        normed = leave2(new, pl.ds(place2(s), edge))

        @pl.when(s == 0)
        def _():
            h2[pl.ds(place2(1), edge)] = normed

        @pl.when(both(s == 1, up))
        def _():
            third.start()

    pl.when(has_last)(second_home.wait_recv)
    leave2(state1[mine] + rest_part(1, h1, home_span), mine)
    pl.when(has_far)(third_home.start)
    relay(2, 1)
    def middle():
        relay(2, 2)

    pl.when(b % 2 == 0)(middle)
    takes(lead)
    leave2_edge(state1[:edge] + rest_part(1, h1, lead_span), lead)
    pl.when(jnp.logical_not(b % 2 == 0))(middle)
    relay(2, 3)

    def last_relays():
        for k in range(4, len(orders[2][0])):
            relay(2, k)
        gather(2, 1)
        gather(2, 0)

    pl.when(b % 2 == 0)(last_relays)

    takes(1 - lead)
    leave2_edge(state1[lead_rows:] + rest_part(1, h1, rear), 1 - lead)
    pl.when(b % 2 == 1)(last_relays)
    finish(2)

    def takes_third(s):
        @pl.when(both(s == 0, down))
        def _():
            third.wait_recv()

    def end_rear():
        now_part(2, u2, rear)
        takes_third(other)
        oback[...] = (state2[lead_rows:] + rest_part(2, h2, rear)).astype(bf16)
        back.start()

    def end_own():
        now_part(2, u2, lead_span)
        takes_third(half)
        out_ref[edge_rows] = (state2[:edge] + rest_part(2, h2, lead_span)).astype(bf16)

    def end_home():
        now_part(2, u2, home_span)
        pl.when(had_far)(third_home.wait_recv)
        out_ref[:part] = (state2[mine] + rest_part(2, h2, home_span)).astype(bf16)

    early = jnp.logical_or(near_cut, both(half == 0, a >= na // 2) | both(half == 1, a >= na // 2))
    pl.when(early)(end_rear)
    end_own()
    pl.when(jnp.logical_not(early))(end_rear)
    end_home()
    for m, there in sent:
        maybe(there, m.wait_send)
    for s in range(2):
        copy, there = second(s)
        pl.when(there)(copy.wait_send)
    pl.when(has_next)(second_home.wait_send)
    pl.when(has_next)(x_next.wait_send)
    pl.when(has_far)(third_home.wait_send)
    pl.when(up)(third.wait_send)
    for c in x_pair:
        c.wait_send()
    back.wait_send()
    back.wait_recv()


def kernel_local(na, nb, sequence_input, w_prev, w_now, conv_bias, w_mix):
    rows, dim = sequence_input.shape
    layers, shard, wide = w_prev.shape
    tail = DILATIONS[0]
    part = 7 * tail // 4
    edge = (rows - part) // 2
    bf16, f32 = jnp.bfloat16, jnp.float32
    halos, copies = 9, 2 * (shard // TILE)
    anywhere = pl.BlockSpec(memory_space=pl.ANY)
    vmem = pl.BlockSpec(memory_space=pltpu.VMEM)
    block = (rows, dim)
    return pl.pallas_call(
        functools.partial(block_kernel, na, nb, part, edge),
        out_shape=pltpu.VMEM((rows, dim), bf16),
        in_specs=[anywhere, anywhere, anywhere, vmem, anywhere],
        out_specs=vmem,
        scratch_shapes=[
            pltpu.VMEM((layers, na, shard, 2 * wide + dim), bf16),
            pltpu.VMEM(block, bf16),
            pltpu.VMEM((tail, dim), bf16),
            pltpu.VMEM((edge + tail, dim), bf16),
            pltpu.VMEM(block, f32),
            pltpu.VMEM(block, f32),
            pltpu.VMEM(block, bf16),
            pltpu.VMEM(block, bf16),
            pltpu.VMEM(block, bf16),
            pltpu.VMEM(block, bf16),
            pltpu.VMEM(block, bf16),
            pltpu.VMEM(block, bf16),
            pltpu.VMEM((rows, wide), f32),
            pltpu.VMEM((edge, dim), bf16),
            pltpu.SemaphoreType.DMA((layers, 3)),
            pltpu.SemaphoreType.DMA,
            pltpu.SemaphoreType.DMA((layers, copies)),
            pltpu.SemaphoreType.DMA((layers, copies)),
            pltpu.SemaphoreType.DMA((halos,)),
            pltpu.SemaphoreType.DMA((halos,)),
            pltpu.SemaphoreType.REGULAR,
        ],
        compiler_params=pltpu.CompilerParams(
            collective_id=0, has_side_effects=True, vmem_limit_bytes=56 * 2**20
        ),
    )(sequence_input, w_prev, w_now, conv_bias, jnp.swapaxes(w_mix, 1, 2))


def local(na, nb, sequence_input, w_prev, w_now, conv_bias, w_mix):
    rows = sequence_input.shape[0]
    shard = w_prev.shape[1]
    fits = (
        na == 4
        and nb % GROUP == 0
        and shard % TILE == 0
        and shard % (2 * TILE) == 0
        and shard >= 10 * TILE
        and rows % (4 * TILE) == 0
        and rows == 4 * DILATIONS[0]
        and DILATIONS[1] == rows
        and 2 * DILATIONS[2] == nb * rows
    )
    body = functools.partial(kernel_local, na, nb) if fits else plain_local
    return body(sequence_input, w_prev, w_now, conv_bias, w_mix)


def solution(mesh):
    return jax.shard_map(
        functools.partial(local, mesh.shape["seqa"], mesh.shape["seqb"]),
        mesh=mesh,
        in_specs=(
            P(("seqa", "seqb"), None),
            P(None, "seqa", None),
            P(None, "seqa", None),
            P(),
            P(None, None, "seqa"),
        ),
        out_specs=P(("seqa", "seqb"), None),
        check_vma=False,
    )
```
